128 devices in a mesh: section: 16 (over z_hi, y, core), rep: 8 (over x, z_lo).
Axes of the slice: x: 4, y: 4, z: 4 (z_hi: 2, z_lo: 2; z = z_hi * 2 + z_lo), core: 2. Of those that a mesh axis runs over, the one named last changes fastest.
Arguments:
- features: bfloat16 [8, 256, 2048], P(None, 'rep'), may hold values from -6 to 6
- positions: int32 [8, 256], P(None, 'rep'), may hold values from 0 to 63
- labels: int32 [8, 256], P(None, 'rep'), may hold values 0 or 1
- cross_u: bfloat16 [2, 16, 2048, 256], P(None, 'section'), may hold values from -0.125 to 0.125
- cross_v: bfloat16 [2, 16, 256, 2048], P(None, 'section'), may hold values from -0.1875 to 0.1875
- cross_bias: float32 [2, 16, 2048], P(None, 'section'), may hold values from -2 to 2
- head: float32 [2048], replicated, may hold values from -0.125 to 0.125
- pos_table: float32 [64, 256], replicated, may hold values from -6 to 6
- debias_hidden_weight: float32 [256, 256], replicated, may hold values from -0.375 to 0.375
- debias_tower_bias: float32 [256], replicated, may hold values from -3 to 3
- debias_output_weight: float32 [256], replicated, may hold values from -0.375 to 0.375
Outputs:
- loss: float32 [], replicated
- grad_u: float32 [2, 16, 2048, 256], P(None, 'section')
- grad_v: float32 [2, 16, 256, 2048], P(None, 'section')
- grad_bias: float32 [2, 16, 2048], P(None, 'section')
The draws below stay inside these ranges and needn't reach their ends.
All inputs are finite; a program needn't handle non-finite values. No bound on the sum of `labels` on one device may be relied on, other than what follows from the above.
Results may differ from the reference program's by a relative error of at most 0.04.
Values may be sent and summed in bfloat16 or wider, within the bound.
No kernel may reach another device: no remote copies, remote signals or barrier semaphores. Data moves between devices by JAX's collectives and lax.ppermute only.
A program may use at most 128 MiB of HBM per device.

```python
import jax
import jax.numpy as jnp
from jax import lax

D = 2048
R = 256
DT = 256
POSN = 64
N_MB = 8
LOOPS = 2
ROWS = 256
N_SECTION = 16


def with_ends(drawn, key, least, largest):
    longest = drawn.shape.index(max(drawn.shape))
    spots = []
    for shift in (0, 1):
        where = [jax.random.randint(jax.random.fold_in(key, axis), (), 0, length) for axis, length in enumerate(drawn.shape)]
        where[longest] = (where[longest] + shift) % drawn.shape[longest]
        spots.append(tuple(where))
    return drawn.at[spots[0]].set(least).at[spots[1]].set(largest)


def levels(rng, dims, cuts, least, top_value):
    factor_of = 1.0
    for position, parts in cuts:
        heights = jax.random.uniform(jax.random.fold_in(jax.random.fold_in(rng, 6), position), (parts,), jnp.float32, least / len(cuts), top_value / len(cuts))
        factor_of = factor_of * jnp.repeat(jnp.exp(heights), dims[position] // parts).reshape((-1,) + (1,) * (len(dims) - 1 - position))
    return factor_of


def gaussian(own_key, shape, scale, most, pieces=(), kind=jnp.bfloat16):
    array = jax.random.normal(own_key, shape, jnp.float32) * scale
    if len(pieces) > 0:
        array = levels(own_key, shape, pieces, -0.22, 0.18) * array
    return jnp.clip(array, min=-most, max=most).astype(kind)


def setup_inputs(seed: int = 0) -> dict:
    streams_of = jax.random.split(jax.random.key(seed), 12)
    features = gaussian(streams_of[0], (N_MB, ROWS, D), 1.0, 6.0, ((1, 8),))
    positions = with_ends(jax.random.randint(streams_of[1], (N_MB, ROWS), 0, POSN), jax.random.fold_in(streams_of[1], 1), 0, POSN - 1).astype(jnp.int32)
    labels = with_ends((jax.random.randint(streams_of[2], (N_MB, ROWS), 0, 4) < 1).astype(jnp.int32), jax.random.fold_in(streams_of[2], 1), 0, 1)
    cross_u = gaussian(streams_of[3], (LOOPS, N_SECTION, D, R), D ** -0.5, 0.125, ((1, 16),))
    cross_v = gaussian(streams_of[4], (LOOPS, N_SECTION, R, D), (4 * R) ** -0.5, 0.1875, ((1, 16),))
    cross_bias = gaussian(streams_of[5], (LOOPS, N_SECTION, D), 0.3, 2.0, ((1, 16),), jnp.float32)
    head = gaussian(streams_of[6], (D,), D ** -0.5, 0.125, (), jnp.float32)
    pos_table = gaussian(streams_of[7], (POSN, DT), 1.0, 6.0, (), jnp.float32)
    debias_hidden_weight = gaussian(streams_of[8], (DT, DT), DT ** -0.5, 0.375, (), jnp.float32)
    debias_tower_bias = gaussian(streams_of[9], (DT,), 0.5, 3.0, (), jnp.float32)
    debias_output_weight = gaussian(streams_of[10], (DT,), DT ** -0.5, 0.375, (), jnp.float32)
    return dict(features=features, positions=positions, labels=labels, cross_u=cross_u, cross_v=cross_v, cross_bias=cross_bias, head=head, pos_table=pos_table, debias_hidden_weight=debias_hidden_weight, debias_tower_bias=debias_tower_bias, debias_output_weight=debias_output_weight)


EPS = 1e-05

def layer_parts(x, x0, w_up, w_down, shift):
    xf = x.astype(jnp.float32)
    scale = lax.rsqrt(lax.optimization_barrier(jnp.mean(xf * xf, axis=-1, keepdims=True)) + EPS)
    normed = (xf * scale).astype(jnp.bfloat16)
    inner = jnp.dot(normed, w_up, preferred_element_type=jnp.float32).astype(jnp.bfloat16)
    cross = jnp.dot(inner, w_down, preferred_element_type=jnp.float32) + shift
    output = (xf + x0.astype(jnp.float32) * cross).astype(jnp.bfloat16)
    return (xf, scale, normed, inner, output)

def layer_back(grad_out, x0, xf, scale, normed, inner, w_up, w_down):
    gcross = (grad_out.astype(jnp.float32) * x0.astype(jnp.float32)).astype(jnp.bfloat16)
    gshift = lax.optimization_barrier(jnp.sum(gcross.astype(jnp.float32), axis=0))
    gdown = jnp.dot(inner.T, gcross, preferred_element_type=jnp.float32)
    ginner = jnp.dot(gcross, w_down.T, preferred_element_type=jnp.float32).astype(jnp.bfloat16)
    gup = jnp.dot(normed.T, ginner, preferred_element_type=jnp.float32)
    gnormed = jnp.dot(ginner, w_up.T, preferred_element_type=jnp.float32)
    gin = grad_out.astype(jnp.float32) + scale * gnormed - xf * scale ** 3 * lax.optimization_barrier(jnp.mean(gnormed * xf, axis=-1, keepdims=True))
    return (gin.astype(jnp.bfloat16), gup, gdown, gshift)

def reference(features, positions, labels, cross_u, cross_v, cross_bias, head, pos_table, debias_hidden_weight, debias_tower_bias, debias_output_weight):
    depth = LOOPS * N_SECTION
    ups = cross_u.reshape(depth, D, R)
    downs = cross_v.reshape(depth, R, D)
    shifts = cross_bias.reshape(depth, D)
    total = N_MB * features.shape[1]
    hidden_index = lax.Precision.HIGHEST

    def micro_step(carry, inputs):
        loss_sum, gu, gv, gb = carry
        x0, pos, lab = inputs

        def forward(x, weights):
            w_up, w_down, shift = weights
            return (layer_parts(x, x0, w_up, w_down, shift)[4], x)
        xl, stash = lax.scan(forward, x0, (ups, downs, shifts))
        onehot = (pos[:, None] == jnp.arange(POSN, dtype=jnp.int32)[None, :]).astype(jnp.float32)
        embedded_rows = jnp.dot(onehot, pos_table, precision=hidden_index)
        hidden_state = jax.nn.relu(jnp.dot(embedded_rows, debias_hidden_weight, precision=hidden_index) + debias_tower_bias)
        click_logit = jnp.dot(xl.astype(jnp.float32), head, precision=hidden_index) + jnp.dot(hidden_state, debias_output_weight, precision=hidden_index)
        labf = lab.astype(jnp.float32)
        loss_part = jnp.sum(jax.nn.softplus(click_logit) - labf * click_logit)
        dlogit = (jax.nn.sigmoid(click_logit) - labf) / total
        dfinal = (dlogit[:, None] * head[None, :]).astype(jnp.bfloat16)

        def backward(grad, weights):
            w_up, w_down, shift, x = weights
            xf, scale, normed, inner, unused = layer_parts(x, x0, w_up, w_down, shift)
            gin, gup, gdown, gshift = layer_back(grad, x0, xf, scale, normed, inner, w_up, w_down)
            return (gin, (gup, gdown, gshift))
        unused_grad, grads = lax.scan(backward, dfinal, (ups, downs, shifts, stash), reverse=True)
        return ((loss_sum + loss_part, gu + grads[0], gv + grads[1], gb + grads[2]), None)
    init = (jnp.zeros((), jnp.float32), jnp.zeros((depth, D, R), jnp.float32), jnp.zeros((depth, R, D), jnp.float32), jnp.zeros((depth, D), jnp.float32))
    result, unused_out = lax.scan(micro_step, init, (features, positions, labels))
    loss_sum, gu, gv, gb = result
    return (loss_sum / total, gu.reshape(LOOPS, N_SECTION, D, R), gv.reshape(LOOPS, N_SECTION, R, D), gb.reshape(LOOPS, N_SECTION, D))
```

```python
import functools

import jax
import jax.numpy as jnp
from jax import lax
from jax.experimental import pallas as pl
from jax.experimental.pallas import tpu as pltpu
from jax.sharding import Mesh
from jax.sharding import PartitionSpec as P

AXES = ("zh", "yp", "yl", "core", "x", "zl")
SECTION = ("zh", "yp", "yl", "core")
REP = ("x", "zl")
EPS = 1e-05
BF = jnp.bfloat16
F32 = jnp.float32
NT = (((1,), (1,)), ((), ()))
TN = (((0,), (0,)), ((), ()))
GROUP = 4
STAGES = 4
PAD = 128


ANY = pl.BlockSpec(memory_space=pltpu.HBM)
VMEM = pl.BlockSpec(memory_space=pltpu.VMEM)


def swap(value, axis):
    return lax.ppermute(value, axis, [(0, 1), (1, 0)])


def y_hop(value):
    return lax.ppermute(value, ("yp", "yl"), [(i, 3 - i) for i in range(4)])


def zy_hop(value):
    return lax.ppermute(value, ("zh", "yp", "yl", "zl"), [(i, 15 - i) for i in range(16)])


def z_align(value):
    return lax.ppermute(value, ("zh", "zl"), [(0, 0), (1, 1), (2, 3), (3, 2)])


def offset_rows(own):
    both = jnp.stack([own, swap(own, "yl")])
    return jnp.stack([both, swap(both, "core")], axis=1)


def flip(layer):
    yl = lax.axis_index("yl")
    core = lax.axis_index("core")
    return lax.rem(layer // 2 + yl, 2) * 2 + lax.rem(layer + core, 2)


def start_weights(loop, pieces, ubuf, vbuf, usem, vsem, order):
    for layer in order:
        k = flip(layer)
        for j in range(GROUP):
            u, v = pieces[j], pieces[GROUP + j]
            if j < 2:
                u, v = u.at[loop], v.at[loop]

            @pl.when(k == j)
            def start(u=u, v=v):
                pltpu.make_async_copy(u, ubuf.at[layer], usem.at[layer]).start()
                pltpu.make_async_copy(v, vbuf.at[layer], vsem.at[layer]).start()


def send_block(buf, outs, sems, layer):
    k = flip(layer)
    for j, out in enumerate(outs):

        @pl.when(k == j)
        def start(out=out):
            pltpu.make_async_copy(buf.at[layer], out, sems.at[layer]).start()


def stage_index():
    return lax.axis_index("zh") * 2 + lax.axis_index("yp")


def forward_kernel(loop, stage, n_alias, x_ref, x0_ref, b_ref, *refs):
    pieces = refs[: 2 * GROUP]
    refs = refs[2 * GROUP + n_alias :]
    out_ref, xs_ref = refs[:2]
    blocks = [ref.at[loop] for ref in refs[2 : 2 + GROUP]]
    ubuf, vbuf, xsbuf, abuf, xbuf, usem, vsem, xsem, asem = refs[2 + GROUP :]
    width = x_ref.shape[1]

    @pl.when(stage_index() == stage)
    def run():
        start_weights(loop, pieces, ubuf, vbuf, usem, vsem, range(GROUP))
        x0 = x0_ref[...].astype(F32)
        xbuf[...] = x_ref[...]

        @pl.loop(0, GROUP)
        def step(layer):
            x = xbuf[...]
            xsbuf[layer] = x
            pltpu.make_async_copy(xsbuf.at[layer], xs_ref.at[layer], xsem.at[layer]).start()
            xf = x.astype(F32)
            scale = lax.rsqrt(jnp.mean(xf * xf, axis=-1, keepdims=True) + EPS)
            normed = (xf * scale).astype(BF)
            abuf[layer, :, 0:width] = normed
            pltpu.make_async_copy(pieces[2], ubuf.at[layer], usem.at[layer]).wait()
            inner = jnp.dot(normed, ubuf[layer], preferred_element_type=F32).astype(BF)
            abuf[layer, :, width:] = inner
            send_block(abuf, blocks, asem, layer)
            pltpu.make_async_copy(pieces[GROUP + 2], vbuf.at[layer], vsem.at[layer]).wait()
            cross = jnp.dot(inner, vbuf[layer], preferred_element_type=F32) + b_ref[pl.ds(flip(layer), 1), :]
            xbuf[...] = (xf + x0 * cross).astype(BF)

        out_ref[...] = xbuf[...]

        @pl.loop(0, GROUP)
        def drain(layer):
            pltpu.make_async_copy(xsbuf.at[layer], xs_ref.at[layer], xsem.at[layer]).wait()
            pltpu.make_async_copy(abuf.at[layer], blocks[0], asem.at[layer]).wait()


def backward_kernel(loop, stage, head_too, total, n_alias, g_ref, x0_ref, xs_ref, *refs):
    pieces = refs[: 2 * GROUP]
    refs = refs[2 * GROUP :]
    if head_too:
        head_ref, extra_ref = refs[:2]
        refs = refs[2:]
    refs = refs[n_alias:]
    out_ref = refs[0]
    refs = refs[1:]
    if head_too:
        logit_ref = refs[0]
        refs = refs[1:]
    blocks = refs[:GROUP]
    ubuf, vbuf, xsbuf, bbuf, gbuf, usem, vsem, xsem, bsem = refs[GROUP:]
    width = g_ref.shape[1]

    @pl.when(stage_index() == stage)
    def run():
        for layer in reversed(range(GROUP)):
            pltpu.make_async_copy(xs_ref.at[layer], xsbuf.at[layer], xsem.at[layer]).start()
        start_weights(loop, pieces, ubuf, vbuf, usem, vsem, reversed(range(GROUP)))
        x0 = x0_ref[...].astype(F32)
        if head_too:
            head = head_ref[...]
            logit = jnp.sum(g_ref[...].astype(F32) * head, axis=-1, keepdims=True) + extra_ref[:, 0:1]
            logit_ref[...] = jnp.broadcast_to(logit, logit_ref.shape)
            dlogit = (jax.nn.sigmoid(logit) - extra_ref[:, 1:2]) / total
            gbuf[...] = (dlogit * head).astype(BF)
        else:
            gbuf[...] = g_ref[...]

        @pl.loop(0, GROUP)
        def step(i):
            layer = GROUP - 1 - i
            g = gbuf[...].astype(F32)
            gcross = (g * x0).astype(BF)
            bbuf[layer, :, 0:width] = gcross
            pltpu.make_async_copy(pieces[GROUP + 2], vbuf.at[layer], vsem.at[layer]).wait()
            ginner = lax.dot_general(gcross, vbuf[layer], NT, preferred_element_type=F32).astype(BF)
            bbuf[layer, :, width:] = ginner
            send_block(bbuf, blocks, bsem, layer)
            pltpu.make_async_copy(pieces[2], ubuf.at[layer], usem.at[layer]).wait()
            gnormed = lax.dot_general(ginner, ubuf[layer], NT, preferred_element_type=F32)
            pltpu.make_async_copy(xs_ref.at[layer], xsbuf.at[layer], xsem.at[layer]).wait()
            xf = xsbuf[layer].astype(F32)
            scale = lax.rsqrt(jnp.mean(xf * xf, axis=-1, keepdims=True) + EPS)
            along = jnp.mean(gnormed * xf, axis=-1, keepdims=True)
            gbuf[...] = (g + scale * gnormed - xf * (scale * scale * scale * along)).astype(BF)

        out_ref[...] = gbuf[...]

        @pl.loop(0, GROUP)
        def drain(layer):
            pltpu.make_async_copy(bbuf.at[layer], blocks[0], bsem.at[layer]).wait()


def run_forward(loop, stage, x, x0, bias, pieces, earlier):
    rows, width = x.shape
    rank = pieces[2].shape[1]
    wide = width + rank
    aliased = () if earlier is None else tuple(earlier)
    block = jax.ShapeDtypeStruct((2, rows, wide), BF)
    outs = pl.pallas_call(
        functools.partial(forward_kernel, loop, stage, len(aliased)),
        out_shape=[jax.ShapeDtypeStruct((rows, width), BF), jax.ShapeDtypeStruct((GROUP, rows, width), BF)]
        + [block] * GROUP,
        in_specs=[VMEM] * 3 + [ANY] * (2 * GROUP + len(aliased)),
        out_specs=[VMEM] + [ANY] * (1 + GROUP),
        scratch_shapes=[
            pltpu.VMEM((GROUP, width, rank), BF),
            pltpu.VMEM((GROUP, rank, width), BF),
            pltpu.VMEM((GROUP, rows, width), BF),
            pltpu.VMEM((GROUP, rows, wide), BF),
            pltpu.VMEM((rows, width), BF),
        ]
        + [pltpu.SemaphoreType.DMA((GROUP,))] * 4,
        input_output_aliases={3 + 2 * GROUP + j: 2 + j for j in range(len(aliased))},
        compiler_params=pltpu.CompilerParams(vmem_limit_bytes=62 << 20),
        cost_estimate=pl.CostEstimate(flops=GROUP * 4 * rows * width * rank, bytes_accessed=GROUP * 4 * width * rank, transcendentals=0),
        name="forward",
    )(x, x0, bias, *pieces, *aliased)
    return outs[0], outs[1], outs[2:]


def run_backward(loop, stage, g, x0, xs, pieces, earlier, total, head=None, extra=None):
    rows, width = g.shape
    rank = pieces[2].shape[1]
    wide = width + rank
    head_too = head is not None
    aliased = () if earlier is None else tuple(earlier)
    block = jax.ShapeDtypeStruct((rows, wide), BF)
    more_in = (head, extra) if head_too else ()
    more_out = [jax.ShapeDtypeStruct((rows, 128), F32)] if head_too else []
    n_out = 1 + len(more_out)
    outs = pl.pallas_call(
        functools.partial(backward_kernel, loop, stage, head_too, total, len(aliased)),
        out_shape=[jax.ShapeDtypeStruct((rows, width), BF)] + more_out + [block] * GROUP,
        in_specs=[VMEM] * 2 + [ANY] * (1 + 2 * GROUP) + [VMEM] * len(more_in) + [ANY] * len(aliased),
        out_specs=[VMEM] * n_out + [ANY] * GROUP,
        scratch_shapes=[
            pltpu.VMEM((GROUP, width, rank), BF),
            pltpu.VMEM((GROUP, rank, width), BF),
            pltpu.VMEM((GROUP, rows, width), BF),
            pltpu.VMEM((GROUP, rows, wide), BF),
            pltpu.VMEM((rows, width), BF),
        ]
        + [pltpu.SemaphoreType.DMA((GROUP,))] * 4,
        input_output_aliases={3 + 2 * GROUP + len(more_in) + j: n_out + j for j in range(len(aliased))},
        compiler_params=pltpu.CompilerParams(vmem_limit_bytes=62 << 20),
        cost_estimate=pl.CostEstimate(flops=GROUP * 4 * rows * width * rank, bytes_accessed=GROUP * 4 * width * rank, transcendentals=0),
        name="backward",
    )(g, x0, xs, *pieces, *more_in, *aliased)
    return outs[0], (outs[1] if head_too else None), outs[n_out:]


def to_owners(blocks):
    cross = lax.ppermute(blocks[3], ("yl", "core"), [(i, 3 - i) for i in range(4)])
    return [blocks[0], swap(blocks[1], "core"), swap(blocks[2], "yl"), cross]


def to_reps(pieces):
    got = []
    for k in range(1, 8):
        dx, dz = k // 2, k % 2
        pairs = [(x * 2 + z, ((x + dx) % 4) * 2 + (z ^ dz)) for x in range(4) for z in range(2)]
        got.append(lax.ppermute(pieces[k - 1], REP, pairs))
    return got


def rep_at(k, sign):
    x = lax.axis_index("x")
    zl = lax.axis_index("zl")
    return lax.rem(x + sign * (k // 2) + 4, 4) * 2 + lax.rem(zl + k % 2, 2)


def aligned(at, size):
    return pl.ds(at if isinstance(at, int) else pl.multiple_of(at, size), size)


def weight_kernel(loop, direct, *refs):
    ablocks, bblocks = [ref.at[loop] for ref in refs[:GROUP]], refs[GROUP : 2 * GROUP]
    an, ai, bc, bg, gu, gv, gb, sem = refs[-8:]
    outs = refs[2 * GROUP : -8]
    rows, width = ablocks[0].shape[0], an.shape[1]
    rank = ai.shape[1]
    copies = []
    for k in range(GROUP):
        at = pl.ds(k * rows, rows)
        for j, (src, cols, dst) in enumerate(
            (
                (ablocks[k], pl.ds(0, width), an),
                (ablocks[k], pl.ds(width, rank), ai),
                (bblocks[k], pl.ds(0, width), bc),
                (bblocks[k], pl.ds(width, rank), bg),
            )
        ):
            copies.append(pltpu.make_async_copy(src.at[:, cols], dst.at[at, :], sem.at[4 * k + j]))
    for copy in copies:
        copy.start()
    for copy in copies:
        copy.wait()
    step = 256

    @pl.loop(0, width // step)
    def up(j):
        cols = pl.ds(pl.multiple_of(j * step, step), step)
        gu[cols, :] = lax.dot_general(an[:, cols], bg[...], TN, preferred_element_type=F32)
        gv[:, cols] = lax.dot_general(ai[...], bc[:, cols], TN, preferred_element_type=F32)

    bias = jnp.sum(bc[...].astype(F32), axis=0, keepdims=True)
    for i in range(width // 128):
        gb[pl.ds(i, 1), :] = bias[:, i * 128 : (i + 1) * 128]
    per_v, per_u = rank // 8, width // 8
    for k in range(8):
        r, out = (rep_at(k, 1), outs[k]) if direct else (k, outs[0].at[k])
        kind = out.dtype
        out[0:per_v, 0:width] = gv[aligned(r * per_v, per_v), :].astype(kind)
        for j in range(per_u // per_v):
            at = aligned(r * per_u + j * per_v, per_v)
            out[per_v : 2 * per_v, j * rank : (j + 1) * rank] = gu[at, :].astype(kind)
        slim = gb[pl.ds(r * 2, 2), :]
        high = slim.astype(kind).astype(F32)
        packed = jnp.concatenate([high, slim - high, jnp.zeros((2 * per_v - 4, PAD), F32)], axis=0)
        out[:, width:] = packed.astype(kind)


def sum_kernel(width, mine, *refs):
    others, out = refs[:7], refs[7]
    total = mine[...]
    for other in others:
        total = total + other[...].astype(F32)
    out[...] = total.astype(BF)
    slim = total[0:2, width:] + total[2:4, width:]
    high = slim.astype(BF).astype(F32)
    packed = jnp.concatenate([high, slim - high, jnp.zeros((total.shape[0] - 4, PAD), F32)], axis=0)
    out[:, width:] = packed.astype(BF)


def spread_kernel(n_alias, *refs):
    gu, gv, gb = refs[-3:]
    pieces = refs[: len(refs) - 3 - n_alias]
    direct = len(pieces) == 8
    rank, width = gv.shape[1:]
    per_v, per_u = rank // 8, width // 8
    for k in range(8):
        r, piece = (rep_at(k, -1), pieces[k]) if direct else (k, pieces[0].at[k])
        gv[0, aligned(r * per_v, per_v), :] = piece[0:per_v, 0:width].astype(F32)
        for j in range(per_u // per_v):
            at = aligned(r * per_u + j * per_v, per_v)
            gu[0, at, :] = piece[per_v : 2 * per_v, j * rank : (j + 1) * rank].astype(F32)
        slim = piece[:, width:].astype(F32)
        gb[0, pl.ds(r * 2, 2), :] = slim[0:2] + slim[2:4]


def weight_gradients(loop, ablocks, bblocks):
    rows, wide = bblocks[0].shape
    rank = 256
    width = wide - rank
    shape = (2 * rank // 8, width + PAD)
    direct = loop == 0
    if direct:
        out_shape = [jax.ShapeDtypeStruct(shape, F32)] + [jax.ShapeDtypeStruct(shape, BF)] * 7
    else:
        out_shape = [jax.ShapeDtypeStruct((8,) + shape, BF)]
    outs = pl.pallas_call(
        functools.partial(weight_kernel, loop, direct),
        out_shape=out_shape,
        in_specs=[ANY] * (2 * GROUP),
        out_specs=[VMEM] * len(out_shape),
        scratch_shapes=[
            pltpu.VMEM((GROUP * rows, width), BF),
            pltpu.VMEM((GROUP * rows, rank), BF),
            pltpu.VMEM((GROUP * rows, width), BF),
            pltpu.VMEM((GROUP * rows, rank), BF),
            pltpu.VMEM((width, rank), F32),
            pltpu.VMEM((rank, width), F32),
            pltpu.VMEM((width // 128, 128), F32),
            pltpu.SemaphoreType.DMA((4 * GROUP,)),
        ],
        compiler_params=pltpu.CompilerParams(vmem_limit_bytes=62 << 20),
        cost_estimate=pl.CostEstimate(flops=4 * GROUP * rows * width * rank, bytes_accessed=4 * GROUP * rows * wide, transcendentals=0),
        name="weights",
    )(*ablocks, *bblocks)
    if not direct:
        return [lax.psum(outs[0], REP)], None
    got = to_reps(outs[1:])
    mine = pl.pallas_call(
        functools.partial(sum_kernel, width),
        out_shape=jax.ShapeDtypeStruct(shape, BF),
        in_specs=[VMEM] * 8,
        out_specs=VMEM,
        compiler_params=pltpu.CompilerParams(vmem_limit_bytes=32 << 20),
        name="total",
    )(outs[0], *got)
    return [mine] + to_reps([mine] * 7), mine


def spread(loop, pieces, earlier, loops, width, rank):
    aliased = () if earlier is None else tuple(earlier)
    shapes = [(loops, width, rank), (loops, rank, width), (loops, width // 128, 128)]
    return pl.pallas_call(
        functools.partial(spread_kernel, len(aliased)),
        grid=(1,),
        out_shape=[jax.ShapeDtypeStruct(s, F32) for s in shapes],
        in_specs=[VMEM] * len(pieces) + [ANY] * len(aliased),
        out_specs=[pl.BlockSpec((1,) + s[1:], lambda i: (loop, 0, 0)) for s in shapes],
        input_output_aliases={len(pieces) + j: j for j in range(len(aliased))},
        compiler_params=pltpu.CompilerParams(vmem_limit_bytes=32 << 20),
        name="spread",
    )(*pieces, *aliased)


def local(features, positions, labels, cross_u, cross_v, cross_bias, head, pos_table, hidden_weight, tower_bias, output_weight):
    w_up, w_down, shifts = cross_u[:, 0], cross_v[:, 0], cross_bias[:, 0]
    loops, width, rank = w_up.shape
    micro, rows = features.shape[:2]
    total = float(micro * rows * 8)
    last = (loops - 1, STAGES - 1)
    yl_rows = lax.rem(lax.axis_index("yl") + lax.axis_index("yp"), 2)
    member = yl_rows * 2 + lax.axis_index("core")
    exact = lax.Precision.HIGHEST
    part = micro // GROUP

    u0, v0 = swap(w_up[0], "yl"), swap(w_down[0], "yl")
    uc, vc = swap(w_up, "core"), swap(w_down, "core")
    up1, down1, u0, v0 = lax.optimization_barrier((w_up[1], w_down[1], u0, v0))
    u1, v1 = swap(up1, "yl"), swap(down1, "yl")
    pieces = [(w_up, uc, u, swap(u, "core"), w_down, vc, v, swap(v, "core")) for u, v in ((u0, v0), (u1, v1))]
    bias = offset_rows(shifts)
    biases = [bias[:, :, j].reshape(GROUP, width) for j in range(loops)]

    def mine(value):
        return lax.dynamic_slice_in_dim(value, member * part, part, 0).reshape((part * rows,) + value.shape[2:])

    x0 = z_align(mine(features))
    onehot = (mine(positions)[:, None] == jnp.arange(pos_table.shape[0], dtype=jnp.int32)).astype(F32)
    embedded = jnp.dot(onehot, pos_table, precision=exact)
    hidden = jax.nn.relu(jnp.dot(embedded, hidden_weight, precision=exact) + tower_bias)
    debias = jnp.dot(hidden, output_weight, precision=exact)
    extra = z_align(jnp.stack([debias, mine(labels).astype(F32)], axis=1))

    x, sent, stash = x0, None, {}
    for loop in range(loops):
        for stage in range(STAGES):
            x, stash[loop, stage], sent = run_forward(loop, stage, x, x0, biases[loop], pieces[loop], sent)
            if (loop, stage) != last:
                x = y_hop(x) if stage % 2 == 0 else zy_hop(x)
    ablocks = to_owners(sent)

    g, grads = x, None
    for loop in reversed(range(loops)):
        sent = None
        for stage in reversed(range(STAGES)):
            more = dict(head=head[None], extra=extra) if (loop, stage) == last else {}
            g, logit, sent = run_backward(loop, stage, g, x0, stash[loop, stage], pieces[loop], sent, total, **more)
            if more:
                logits = logit[:, 0]
            if (loop, stage) != (0, 0):
                g = y_hop(g) if stage % 2 == 1 else zy_hop(g)
        reduced, late = weight_gradients(loop, ablocks, to_owners(sent))
        grads = spread(loop, reduced, grads, loops, width, rank)
    loss_part = jnp.sum(jax.nn.softplus(logits) - extra[:, 1] * logits)
    loss_part = jnp.where(stage_index() == STAGES - 1, loss_part, 0.0)
    loss, _ = lax.optimization_barrier((loss_part, late))
    for axes in ("zh", ("yp", "yl"), "core", "x", "zl"):
        loss = lax.psum(loss, axes)
    loss = loss / total
    gu, gv, gb = grads
    return loss, gu[:, None], gv[:, None], gb.reshape(loops, 1, width)


def solution(mesh):
    finer = Mesh(mesh.devices.reshape(2, 2, 2, 2, 4, 2), AXES)
    placed = (
        P(None, REP, None),
        P(None, REP),
        P(None, REP),
        P(None, SECTION, None, None),
        P(None, SECTION, None, None),
        P(None, SECTION, None),
        P(),
        P(),
        P(),
        P(),
        P(),
    )
    return jax.shard_map(
        local,
        mesh=finer,
        in_specs=placed,
        out_specs=(P(), P(None, SECTION, None, None), P(None, SECTION, None, None), P(None, SECTION, None)),
        check_vma=False,
    )
```

```python
import functools

import jax
import jax.numpy as jnp
from jax import lax
from jax.experimental import pallas as pl
from jax.experimental.pallas import tpu as pltpu
from jax.sharding import Mesh
from jax.sharding import PartitionSpec as P

AXES = ("zh", "yp", "yl", "core", "x", "zl")
SECTION = ("zh", "yp", "yl", "core")
REP = ("x", "zl")
EPS = 1e-05
BF = jnp.bfloat16
F32 = jnp.float32
NT = (((1,), (1,)), ((), ()))
TN = (((0,), (0,)), ((), ()))
GROUP = 4
STAGES = 4
PAD = 128
FWD_MIB = 8


ANY = pl.BlockSpec(memory_space=pltpu.HBM)
VMEM = pl.BlockSpec(memory_space=pltpu.VMEM)


def swap(value, axis):
    return lax.ppermute(value, axis, [(0, 1), (1, 0)])


def y_hop(value):
    return lax.ppermute(value, ("yp", "yl"), [(i, 3 - i) for i in range(4)])


def zy_hop(value):
    return lax.ppermute(value, ("zh", "yp", "yl", "zl"), [(i, 15 - i) for i in range(16)])


def z_align(value):
    return lax.ppermute(value, ("zh", "zl"), [(0, 0), (1, 1), (2, 3), (3, 2)])


def offset_rows(own):
    both = jnp.stack([own, swap(own, "yl")])
    return jnp.stack([both, swap(both, "core")], axis=1)


def flip(layer):
    yl = lax.axis_index("yl")
    core = lax.axis_index("core")
    return lax.rem(layer // 2 + yl, 2) * 2 + lax.rem(layer + core, 2)


def assemble_kernel(loop, *refs):
    pieces = refs[: 2 * GROUP]
    u_ref, v_ref, usem, vsem = refs[2 * GROUP :]
    for layer in range(GROUP):
        k = flip(layer)
        for j in range(GROUP):
            u, v = pieces[j], pieces[GROUP + j]
            if j < 2:
                u, v = u.at[loop], v.at[loop]

            @pl.when(k == j)
            def start(u=u, v=v):
                pltpu.make_async_copy(u, u_ref.at[layer], usem.at[layer]).start()
                pltpu.make_async_copy(v, v_ref.at[layer], vsem.at[layer]).start()

    for layer in range(GROUP):
        pltpu.make_async_copy(pieces[2], u_ref.at[layer], usem.at[layer]).wait()
        pltpu.make_async_copy(pieces[GROUP + 2], v_ref.at[layer], vsem.at[layer]).wait()


def assemble(loop, pieces):
    width, rank = pieces[2].shape
    return pl.pallas_call(
        functools.partial(assemble_kernel, loop),
        out_shape=[jax.ShapeDtypeStruct((GROUP, width, rank), BF), jax.ShapeDtypeStruct((GROUP, rank, width), BF)],
        in_specs=[ANY] * (2 * GROUP),
        out_specs=[VMEM] * 2,
        scratch_shapes=[pltpu.SemaphoreType.DMA((GROUP,))] * 2,
        compiler_params=pltpu.CompilerParams(vmem_limit_bytes=12 << 20),
        cost_estimate=pl.CostEstimate(flops=0, bytes_accessed=GROUP * 4 * width * rank, transcendentals=0),
        name="assemble",
    )(*pieces)


def send_block(buf, outs, sems, layer):
    k = flip(layer)
    for j, out in enumerate(outs):

        @pl.when(k == j)
        def start(out=out):
            pltpu.make_async_copy(buf.at[layer], out, sems.at[layer]).start()


def stage_index():
    return lax.axis_index("zh") * 2 + lax.axis_index("yp")


def forward_kernel(loop, stage, n_alias, x_ref, x0_ref, b_ref, *refs):
    u_ref, v_ref = refs[:2]
    refs = refs[2 + n_alias :]
    out_ref, xs_ref = refs[:2]
    blocks = [ref.at[loop] for ref in refs[2 : 2 + GROUP]]
    xsbuf, abuf, xbuf, x0buf, bbuf, xsem, asem, sem = refs[2 + GROUP :]
    width = x_ref.shape[1]

    @pl.when(stage_index() == stage)
    def run():
        copies = [pltpu.make_async_copy(src, dst, sem.at[i]) for i, (src, dst) in enumerate(((x_ref, xbuf), (x0_ref, x0buf), (b_ref, bbuf)))]
        for copy in copies:
            copy.start()
        for copy in copies:
            copy.wait()

        @pl.loop(0, GROUP)
        def step(layer):
            x = xbuf[...]
            xsbuf[layer] = x
            pltpu.make_async_copy(xsbuf.at[layer], xs_ref.at[layer], xsem.at[layer]).start()
            xf = x.astype(F32)
            scale = lax.rsqrt(jnp.mean(xf * xf, axis=-1, keepdims=True) + EPS)
            normed = (xf * scale).astype(BF)
            abuf[layer, :, 0:width] = normed
            inner = jnp.dot(normed, u_ref[layer], preferred_element_type=F32).astype(BF)
            abuf[layer, :, width:] = inner
            send_block(abuf, blocks, asem, layer)
            cross = jnp.dot(inner, v_ref[layer], preferred_element_type=F32) + bbuf[pl.ds(flip(layer), 1), :]
            xbuf[...] = (xf + x0buf[...].astype(F32) * cross).astype(BF)

        out_ref[...] = xbuf[...]

        @pl.loop(0, GROUP)
        def drain(layer):
            pltpu.make_async_copy(xsbuf.at[layer], xs_ref.at[layer], xsem.at[layer]).wait()
            pltpu.make_async_copy(abuf.at[layer], blocks[0], asem.at[layer]).wait()


def backward_kernel(loop, stage, head_too, total, n_alias, g_ref, x0_ref, xs_ref, *refs):
    u_ref, v_ref = refs[:2]
    refs = refs[2:]
    if head_too:
        head_ref, extra_ref = refs[:2]
        refs = refs[2:]
    refs = refs[n_alias:]
    out_ref = refs[0]
    refs = refs[1:]
    if head_too:
        logit_ref = refs[0]
        refs = refs[1:]
    blocks = refs[:GROUP]
    xsbuf, bbuf, gbuf, x0buf, xsem, bsem, sem = refs[GROUP:]
    width = g_ref.shape[1]

    @pl.when(stage_index() == stage)
    def run():
        copies = [pltpu.make_async_copy(g_ref, gbuf, sem.at[0]), pltpu.make_async_copy(x0_ref, x0buf, sem.at[1])]
        for copy in copies:
            copy.start()
        for layer in reversed(range(GROUP)):
            pltpu.make_async_copy(xs_ref.at[layer], xsbuf.at[layer], xsem.at[layer]).start()
        for copy in copies:
            copy.wait()
        if head_too:
            head = head_ref[...]
            logit = jnp.sum(gbuf[...].astype(F32) * head, axis=-1, keepdims=True) + extra_ref[:, 0:1]
            logit_ref[...] = jnp.broadcast_to(logit, logit_ref.shape)
            dlogit = (jax.nn.sigmoid(logit) - extra_ref[:, 1:2]) / total
            gbuf[...] = (dlogit * head).astype(BF)

        @pl.loop(0, GROUP)
        def step(i):
            layer = GROUP - 1 - i
            g = gbuf[...].astype(F32)
            gcross = (g * x0buf[...].astype(F32)).astype(BF)
            bbuf[layer, :, 0:width] = gcross
            ginner = lax.dot_general(gcross, v_ref[layer], NT, preferred_element_type=F32).astype(BF)
            bbuf[layer, :, width:] = ginner
            send_block(bbuf, blocks, bsem, layer)
            gnormed = lax.dot_general(ginner, u_ref[layer], NT, preferred_element_type=F32)
            pltpu.make_async_copy(xs_ref.at[layer], xsbuf.at[layer], xsem.at[layer]).wait()
            xf = xsbuf[layer].astype(F32)
            scale = lax.rsqrt(jnp.mean(xf * xf, axis=-1, keepdims=True) + EPS)
            along = jnp.mean(gnormed * xf, axis=-1, keepdims=True)
            gbuf[...] = (g + scale * gnormed - xf * (scale * scale * scale * along)).astype(BF)

        out_ref[...] = gbuf[...]

        @pl.loop(0, GROUP)
        def drain(layer):
            pltpu.make_async_copy(bbuf.at[layer], blocks[0], bsem.at[layer]).wait()


def run_forward(loop, stage, x, x0, bias, pieces, earlier):
    rows, width = x.shape
    rank = pieces[1].shape[1]
    wide = width + rank
    aliased = () if earlier is None else tuple(earlier)
    block = jax.ShapeDtypeStruct((2, rows, wide), BF)
    outs = pl.pallas_call(
        functools.partial(forward_kernel, loop, stage, len(aliased)),
        out_shape=[jax.ShapeDtypeStruct((rows, width), BF), jax.ShapeDtypeStruct((GROUP, rows, width), BF)]
        + [block] * GROUP,
        in_specs=[ANY] * 3 + [VMEM] * 2 + [ANY] * len(aliased),
        out_specs=[VMEM] + [ANY] * (1 + GROUP),
        scratch_shapes=[
            pltpu.VMEM((GROUP, rows, width), BF),
            pltpu.VMEM((GROUP, rows, wide), BF),
            pltpu.VMEM((rows, width), BF),
            pltpu.VMEM((rows, width), BF),
            pltpu.VMEM((GROUP, width), F32),
        ]
        + [pltpu.SemaphoreType.DMA((GROUP,))] * 3,
        input_output_aliases={5 + j: 2 + j for j in range(len(aliased))},
        compiler_params=pltpu.CompilerParams(vmem_limit_bytes=FWD_MIB << 20),
        cost_estimate=pl.CostEstimate(flops=GROUP * 4 * rows * width * rank, bytes_accessed=GROUP * 4 * width * rank, transcendentals=0),
        name="forward",
    )(x, x0, bias, *pieces, *aliased)
    return outs[0], outs[1], outs[2:]


def run_backward(loop, stage, g, x0, xs, pieces, earlier, total, head=None, extra=None):
    rows, width = g.shape
    rank = pieces[1].shape[1]
    wide = width + rank
    head_too = head is not None
    aliased = () if earlier is None else tuple(earlier)
    block = jax.ShapeDtypeStruct((rows, wide), BF)
    more_in = (head, extra) if head_too else ()
    more_out = [jax.ShapeDtypeStruct((rows, 128), F32)] if head_too else []
    n_out = 1 + len(more_out)
    outs = pl.pallas_call(
        functools.partial(backward_kernel, loop, stage, head_too, total, len(aliased)),
        out_shape=[jax.ShapeDtypeStruct((rows, width), BF)] + more_out + [block] * GROUP,
        in_specs=[ANY] * 3 + [VMEM] * (2 + len(more_in)) + [ANY] * len(aliased),
        out_specs=[VMEM] * n_out + [ANY] * GROUP,
        scratch_shapes=[
            pltpu.VMEM((GROUP, rows, width), BF),
            pltpu.VMEM((GROUP, rows, wide), BF),
            pltpu.VMEM((rows, width), BF),
            pltpu.VMEM((rows, width), BF),
        ]
        + [pltpu.SemaphoreType.DMA((GROUP,))] * 3,
        input_output_aliases={5 + len(more_in) + j: n_out + j for j in range(len(aliased))},
        compiler_params=pltpu.CompilerParams(vmem_limit_bytes=FWD_MIB << 20),
        cost_estimate=pl.CostEstimate(flops=GROUP * 4 * rows * width * rank, bytes_accessed=GROUP * 4 * width * rank, transcendentals=0),
        name="backward",
    )(g, x0, xs, *pieces, *more_in, *aliased)
    return outs[0], (outs[1] if head_too else None), outs[n_out:]


def to_owners(blocks):
    cross = lax.ppermute(blocks[3], ("yl", "core"), [(i, 3 - i) for i in range(4)])
    return [blocks[0], swap(blocks[1], "core"), swap(blocks[2], "yl"), cross]


def to_reps(pieces):
    got = []
    for k in range(1, 8):
        dx, dz = k // 2, k % 2
        pairs = [(x * 2 + z, ((x + dx) % 4) * 2 + (z ^ dz)) for x in range(4) for z in range(2)]
        got.append(lax.ppermute(pieces[k - 1], REP, pairs))
    return got


def rep_at(k, sign):
    x = lax.axis_index("x")
    zl = lax.axis_index("zl")
    return lax.rem(x + sign * (k // 2) + 4, 4) * 2 + lax.rem(zl + k % 2, 2)


def aligned(at, size):
    return pl.ds(at if isinstance(at, int) else pl.multiple_of(at, size), size)


def weight_kernel(loop, direct, *refs):
    ablocks, bblocks = [ref.at[loop] for ref in refs[:GROUP]], refs[GROUP : 2 * GROUP]
    an, ai, bc, bg, gu, gv, gb, sem = refs[-8:]
    outs = refs[2 * GROUP : -8]
    rows, width = ablocks[0].shape[0], an.shape[1]
    rank = ai.shape[1]
    copies = []
    for k in range(GROUP):
        at = pl.ds(k * rows, rows)
        for j, (src, cols, dst) in enumerate(
            (
                (ablocks[k], pl.ds(0, width), an),
                (ablocks[k], pl.ds(width, rank), ai),
                (bblocks[k], pl.ds(0, width), bc),
                (bblocks[k], pl.ds(width, rank), bg),
            )
        ):
            copies.append(pltpu.make_async_copy(src.at[:, cols], dst.at[at, :], sem.at[4 * k + j]))
    for copy in copies:
        copy.start()
    for copy in copies:
        copy.wait()
    step = 256

    @pl.loop(0, width // step)
    def up(j):
        cols = pl.ds(pl.multiple_of(j * step, step), step)
        gu[cols, :] = lax.dot_general(an[:, cols], bg[...], TN, preferred_element_type=F32)
        gv[:, cols] = lax.dot_general(ai[...], bc[:, cols], TN, preferred_element_type=F32)

    bias = jnp.sum(bc[...].astype(F32), axis=0, keepdims=True)
    for i in range(width // 128):
        gb[pl.ds(i, 1), :] = bias[:, i * 128 : (i + 1) * 128]
    per_v, per_u = rank // 8, width // 8
    for k in range(8):
        r, out = (rep_at(k, 1), outs[k]) if direct else (k, outs[0].at[k])
        kind = out.dtype
        out[0:per_v, 0:width] = gv[aligned(r * per_v, per_v), :].astype(kind)
        for j in range(per_u // per_v):
            at = aligned(r * per_u + j * per_v, per_v)
            out[per_v : 2 * per_v, j * rank : (j + 1) * rank] = gu[at, :].astype(kind)
        slim = gb[pl.ds(r * 2, 2), :]
        high = slim.astype(kind).astype(F32)
        packed = jnp.concatenate([high, slim - high, jnp.zeros((2 * per_v - 4, PAD), F32)], axis=0)
        out[:, width:] = packed.astype(kind)


def sum_kernel(width, mine, *refs):
    others, out = refs[:7], refs[7]
    total = mine[...]
    for other in others:
        total = total + other[...].astype(F32)
    out[...] = total.astype(BF)
    slim = total[0:2, width:] + total[2:4, width:]
    high = slim.astype(BF).astype(F32)
    packed = jnp.concatenate([high, slim - high, jnp.zeros((total.shape[0] - 4, PAD), F32)], axis=0)
    out[:, width:] = packed.astype(BF)


def spread_kernel(n_alias, *refs):
    gu, gv, gb = refs[-3:]
    pieces = refs[: len(refs) - 3 - n_alias]
    direct = len(pieces) == 8
    rank, width = gv.shape[1:]
    per_v, per_u = rank // 8, width // 8
    for k in range(8):
        r, piece = (rep_at(k, -1), pieces[k]) if direct else (k, pieces[0].at[k])
        gv[0, aligned(r * per_v, per_v), :] = piece[0:per_v, 0:width].astype(F32)
        for j in range(per_u // per_v):
            at = aligned(r * per_u + j * per_v, per_v)
            gu[0, at, :] = piece[per_v : 2 * per_v, j * rank : (j + 1) * rank].astype(F32)
        slim = piece[:, width:].astype(F32)
        gb[0, pl.ds(r * 2, 2), :] = slim[0:2] + slim[2:4]


def weight_gradients(loop, ablocks, bblocks, loss):
    rows, wide = bblocks[0].shape
    rank = 256
    width = wide - rank
    shape = (2 * rank // 8, width + PAD)
    direct = loop == 0
    if direct:
        out_shape = [jax.ShapeDtypeStruct(shape, F32)] + [jax.ShapeDtypeStruct(shape, BF)] * 7
    else:
        out_shape = [jax.ShapeDtypeStruct((8,) + shape, BF)]
    outs = pl.pallas_call(
        functools.partial(weight_kernel, loop, direct),
        out_shape=out_shape,
        in_specs=[ANY] * (2 * GROUP),
        out_specs=[VMEM] * len(out_shape),
        scratch_shapes=[
            pltpu.VMEM((GROUP * rows, width), BF),
            pltpu.VMEM((GROUP * rows, rank), BF),
            pltpu.VMEM((GROUP * rows, width), BF),
            pltpu.VMEM((GROUP * rows, rank), BF),
            pltpu.VMEM((width, rank), F32),
            pltpu.VMEM((rank, width), F32),
            pltpu.VMEM((width // 128, 128), F32),
            pltpu.SemaphoreType.DMA((4 * GROUP,)),
        ],
        compiler_params=pltpu.CompilerParams(vmem_limit_bytes=14 << 20),
        cost_estimate=pl.CostEstimate(flops=4 * GROUP * rows * width * rank, bytes_accessed=4 * GROUP * rows * wide, transcendentals=0),
        name="weights",
    )(*ablocks, *bblocks)
    if not direct:
        return [lax.psum(outs[0], REP)], None
    outs, loss = lax.optimization_barrier((list(outs), loss))
    for axes in (("yp", "yl"), "core"):
        loss = lax.psum(loss, axes)
    got = to_reps(outs[1:])
    mine = pl.pallas_call(
        functools.partial(sum_kernel, width),
        out_shape=jax.ShapeDtypeStruct(shape, BF),
        in_specs=[VMEM] * 8,
        out_specs=VMEM,
        compiler_params=pltpu.CompilerParams(vmem_limit_bytes=16 << 20),
        name="total",
    )(outs[0], *got)
    return [mine] + to_reps([mine] * 7), loss


def spread(loop, pieces, earlier, loops, width, rank):
    aliased = () if earlier is None else tuple(earlier)
    shapes = [(loops, width, rank), (loops, rank, width), (loops, width // 128, 128)]
    return pl.pallas_call(
        functools.partial(spread_kernel, len(aliased)),
        grid=(1,),
        out_shape=[jax.ShapeDtypeStruct(s, F32) for s in shapes],
        in_specs=[VMEM] * len(pieces) + [ANY] * len(aliased),
        out_specs=[pl.BlockSpec((1,) + s[1:], lambda i: (loop, 0, 0)) for s in shapes],
        input_output_aliases={len(pieces) + j: j for j in range(len(aliased))},
        compiler_params=pltpu.CompilerParams(vmem_limit_bytes=16 << 20),
        name="spread",
    )(*pieces, *aliased)


def local(features, positions, labels, cross_u, cross_v, cross_bias, head, pos_table, hidden_weight, tower_bias, output_weight):
    w_up, w_down, shifts = cross_u[:, 0], cross_v[:, 0], cross_bias[:, 0]
    loops, width, rank = w_up.shape
    micro, rows = features.shape[:2]
    total = float(micro * rows * 8)
    last = (loops - 1, STAGES - 1)
    yl_rows = lax.rem(lax.axis_index("yl") + lax.axis_index("yp"), 2)
    member = yl_rows * 2 + lax.axis_index("core")
    exact = lax.Precision.HIGHEST
    part = micro // GROUP

    u0, v0 = swap(w_up[0], "yl"), swap(w_down[0], "yl")
    uc, vc = swap(w_up, "core"), swap(w_down, "core")
    bias = offset_rows(shifts)
    def mine(value):
        return lax.dynamic_slice_in_dim(value, member * part, part, 0).reshape((part * rows,) + value.shape[2:])

    x0 = z_align(mine(features))
    onehot = (mine(positions)[:, None] == jnp.arange(pos_table.shape[0], dtype=jnp.int32)).astype(F32)
    embedded = jnp.dot(onehot, pos_table, precision=exact)
    hidden = jax.nn.relu(jnp.dot(embedded, hidden_weight, precision=exact) + tower_bias)
    debias = jnp.dot(hidden, output_weight, precision=exact)
    extra = z_align(jnp.stack([debias, mine(labels).astype(F32)], axis=1))
    biases = [bias[:, :, j].reshape(GROUP, width) for j in range(loops)]
    head = head[None]
    up1, down1, u0, v0, biases, x0, extra, head = lax.optimization_barrier((w_up, w_down, u0, v0, biases, x0, extra, head))
    u1, v1 = swap(up1[1], "yl"), swap(down1[1], "yl")

    def pieces_of(loop, u, v):
        return assemble(loop, (w_up, uc, u, swap(u, "core"), w_down, vc, v, swap(v, "core")))

    pieces = [pieces_of(0, u0, v0)]
    x, sent, stash = x0, None, {}
    for loop in range(loops):
        for stage in range(STAGES):
            x, stash[loop, stage], sent = run_forward(loop, stage, x, x0, biases[loop], pieces[loop], sent)
            if (loop, stage) == (0, 2):
                u1, v1, x = lax.optimization_barrier((u1, v1, x))
                pieces.append(pieces_of(1, u1, v1))
            if (loop, stage) != last:
                x = y_hop(x) if stage % 2 == 0 else zy_hop(x)
    ablocks = to_owners(sent)

    g = x
    for loop in reversed(range(loops)):
        sent = None
        for stage in reversed(range(STAGES)):
            more = dict(head=head, extra=extra) if (loop, stage) == last else {}
            g, logit, sent = run_backward(loop, stage, g, x0, stash[loop, stage], pieces[loop], sent, total, **more)
            if more:
                logits = logit[:, 0]
            if (loop, stage) == (1, 1):
                ablocks, g = lax.optimization_barrier((ablocks, g))
            if (loop, stage) == (0, STAGES - 2):
                bblocks, g = lax.optimization_barrier((bblocks, g))
                upper, _ = weight_gradients(1, ablocks, bblocks, None)
            if (loop, stage) != (0, 0):
                g = y_hop(g) if stage % 2 == 1 else zy_hop(g)
        if loop == 0:
            sent, logits = lax.optimization_barrier((sent, logits))
            loss = jnp.sum(jax.nn.softplus(logits) - extra[:, 1] * logits)
            loss = jnp.where(stage_index() == STAGES - 1, loss, 0.0)
        bblocks = to_owners(sent)
    loss = lax.psum(lax.psum(loss, ("zh", "zl")), "x")
    lower, loss = weight_gradients(0, ablocks, bblocks, loss)
    grads = spread(0, lower, spread(1, upper, None, loops, width, rank), loops, width, rank)
    loss = loss / total
    gu, gv, gb = grads
    return loss, gu[:, None], gv[:, None], gb.reshape(loops, 1, width)


def solution(mesh):
    finer = Mesh(mesh.devices.reshape(2, 2, 2, 2, 4, 2), AXES)
    placed = (
        P(None, REP, None),
        P(None, REP),
        P(None, REP),
        P(None, SECTION, None, None),
        P(None, SECTION, None, None),
        P(None, SECTION, None),
        P(),
        P(),
        P(),
        P(),
        P(),
    )
    return jax.shard_map(
        local,
        mesh=finer,
        in_specs=placed,
        out_specs=(P(), P(None, SECTION, None, None), P(None, SECTION, None, None), P(None, SECTION, None)),
        check_vma=False,
    )
```

```python
import functools

import jax
import jax.numpy as jnp
from jax import lax
from jax.experimental import pallas as pl
from jax.experimental.pallas import tpu as pltpu
from jax.sharding import Mesh
from jax.sharding import PartitionSpec as P

AXES = ("zh", "yp", "yl", "core", "x", "zl")
SECTION = ("zh", "yp", "yl", "core")
REP = ("x", "zl")
EPS = 1e-05
BF = jnp.bfloat16
F32 = jnp.float32
NT = (((1,), (1,)), ((), ()))
TN = (((0,), (0,)), ((), ()))
GROUP = 4
STAGES = 4
PAD = 128
FWD_MIB = 8


ANY = pl.BlockSpec(memory_space=pltpu.HBM)
VMEM = pl.BlockSpec(memory_space=pltpu.VMEM)


def swap(value, axis):
    return lax.ppermute(value, axis, [(0, 1), (1, 0)])


def y_hop(value):
    return lax.ppermute(value, ("yp", "yl"), [(i, 3 - i) for i in range(4)])


def zy_hop(value):
    return lax.ppermute(value, ("zh", "yp", "yl", "zl"), [(i, 15 - i) for i in range(16)])


def z_align(value):
    return lax.ppermute(value, ("zh", "zl"), [(0, 0), (1, 1), (2, 3), (3, 2)])


def offset_rows(own):
    both = jnp.stack([own, swap(own, "yl")])
    return jnp.stack([both, swap(both, "core")], axis=1)


def flip(layer):
    yl = lax.axis_index("yl")
    core = lax.axis_index("core")
    return lax.rem(layer // 2 + yl, 2) * 2 + lax.rem(layer + core, 2)


def assemble_kernel(loop, *refs):
    pieces = refs[: 2 * GROUP]
    u_ref, v_ref, usem, vsem = refs[2 * GROUP :]
    for layer in range(GROUP):
        k = flip(layer)
        for j in range(GROUP):
            u, v = pieces[j], pieces[GROUP + j]
            if j < 2:
                u, v = u.at[loop], v.at[loop]

            @pl.when(k == j)
            def start(u=u, v=v):
                pltpu.make_async_copy(u, u_ref.at[layer], usem.at[layer]).start()
                pltpu.make_async_copy(v, v_ref.at[layer], vsem.at[layer]).start()

    for layer in range(GROUP):
        pltpu.make_async_copy(pieces[2], u_ref.at[layer], usem.at[layer]).wait()
        pltpu.make_async_copy(pieces[GROUP + 2], v_ref.at[layer], vsem.at[layer]).wait()


def assemble(loop, pieces):
    width, rank = pieces[2].shape
    return pl.pallas_call(
        functools.partial(assemble_kernel, loop),
        out_shape=[jax.ShapeDtypeStruct((GROUP, width, rank), BF), jax.ShapeDtypeStruct((GROUP, rank, width), BF)],
        in_specs=[ANY] * (2 * GROUP),
        out_specs=[VMEM] * 2,
        scratch_shapes=[pltpu.SemaphoreType.DMA((GROUP,))] * 2,
        compiler_params=pltpu.CompilerParams(vmem_limit_bytes=12 << 20),
        cost_estimate=pl.CostEstimate(flops=0, bytes_accessed=GROUP * 4 * width * rank, transcendentals=0),
        name="assemble",
    )(*pieces)


def send_block(buf, outs, sems, layer):
    k = flip(layer)
    for j, out in enumerate(outs):

        @pl.when(k == j)
        def start(out=out):
            pltpu.make_async_copy(buf.at[layer], out, sems.at[layer]).start()


def stage_index():
    return lax.axis_index("zh") * 2 + lax.axis_index("yp")


def forward_kernel(loop, stage, n_alias, x_ref, x0_ref, b_ref, *refs):
    u_ref, v_ref = refs[:2]
    refs = refs[2 + n_alias :]
    out_ref, xs_ref = refs[:2]
    blocks = [ref.at[loop] for ref in refs[2 : 2 + GROUP]]
    xsbuf, abuf, xbuf, x0buf, bbuf, xsem, asem, sem = refs[2 + GROUP :]
    width = x_ref.shape[1]

    @pl.when(stage_index() == stage)
    def run():
        copies = [pltpu.make_async_copy(src, dst, sem.at[i]) for i, (src, dst) in enumerate(((x_ref, xbuf), (x0_ref, x0buf), (b_ref, bbuf)))]
        for copy in copies:
            copy.start()
        for copy in copies:
            copy.wait()

        @pl.loop(0, GROUP)
        def step(layer):
            x = xbuf[...]
            xsbuf[layer] = x
            pltpu.make_async_copy(xsbuf.at[layer], xs_ref.at[layer], xsem.at[layer]).start()
            xf = x.astype(F32)
            scale = lax.rsqrt(jnp.mean(xf * xf, axis=-1, keepdims=True) + EPS)
            normed = (xf * scale).astype(BF)
            abuf[layer, :, 0:width] = normed
            inner = jnp.dot(normed, u_ref[layer], preferred_element_type=F32).astype(BF)
            abuf[layer, :, width:] = inner
            send_block(abuf, blocks, asem, layer)
            cross = jnp.dot(inner, v_ref[layer], preferred_element_type=F32) + bbuf[pl.ds(flip(layer), 1), :]
            xbuf[...] = (xf + x0buf[...].astype(F32) * cross).astype(BF)

        out_ref[...] = xbuf[...]

        @pl.loop(0, GROUP)
        def drain(layer):
            pltpu.make_async_copy(xsbuf.at[layer], xs_ref.at[layer], xsem.at[layer]).wait()
            pltpu.make_async_copy(abuf.at[layer], blocks[0], asem.at[layer]).wait()


def backward_kernel(loop, stage, head_too, total, n_alias, g_ref, x0_ref, xs_ref, *refs):
    u_ref, v_ref = refs[:2]
    refs = refs[2:]
    if head_too:
        head_ref, extra_ref = refs[:2]
        refs = refs[2:]
    refs = refs[n_alias:]
    out_ref = refs[0]
    refs = refs[1:]
    if head_too:
        logit_ref = refs[0]
        refs = refs[1:]
    blocks = refs[:GROUP]
    xsbuf, bbuf, gbuf, x0buf, xsem, bsem, sem = refs[GROUP:]
    width = g_ref.shape[1]

    @pl.when(stage_index() == stage)
    def run():
        copies = [pltpu.make_async_copy(g_ref, gbuf, sem.at[0]), pltpu.make_async_copy(x0_ref, x0buf, sem.at[1])]
        for copy in copies:
            copy.start()
        for layer in reversed(range(GROUP)):
            pltpu.make_async_copy(xs_ref.at[layer], xsbuf.at[layer], xsem.at[layer]).start()
        for copy in copies:
            copy.wait()
        if head_too:
            head = head_ref[...]
            logit = jnp.sum(gbuf[...].astype(F32) * head, axis=-1, keepdims=True) + extra_ref[:, 0:1]
            logit_ref[...] = jnp.broadcast_to(logit, logit_ref.shape)
            dlogit = (jax.nn.sigmoid(logit) - extra_ref[:, 1:2]) / total
            gbuf[...] = (dlogit * head).astype(BF)

        @pl.loop(0, GROUP)
        def step(i):
            layer = GROUP - 1 - i
            g = gbuf[...].astype(F32)
            gcross = (g * x0buf[...].astype(F32)).astype(BF)
            bbuf[layer, :, 0:width] = gcross
            ginner = lax.dot_general(gcross, v_ref[layer], NT, preferred_element_type=F32).astype(BF)
            bbuf[layer, :, width:] = ginner
            send_block(bbuf, blocks, bsem, layer)
            gnormed = lax.dot_general(ginner, u_ref[layer], NT, preferred_element_type=F32)
            pltpu.make_async_copy(xs_ref.at[layer], xsbuf.at[layer], xsem.at[layer]).wait()
            xf = xsbuf[layer].astype(F32)
            scale = lax.rsqrt(jnp.mean(xf * xf, axis=-1, keepdims=True) + EPS)
            along = jnp.mean(gnormed * xf, axis=-1, keepdims=True)
            gbuf[...] = (g + scale * gnormed - xf * (scale * scale * scale * along)).astype(BF)

        out_ref[...] = gbuf[...]

        @pl.loop(0, GROUP)
        def drain(layer):
            pltpu.make_async_copy(bbuf.at[layer], blocks[0], bsem.at[layer]).wait()


def run_forward(loop, stage, x, x0, bias, pieces, earlier):
    rows, width = x.shape
    rank = pieces[1].shape[1]
    wide = width + rank
    aliased = () if earlier is None else tuple(earlier)
    block = jax.ShapeDtypeStruct((2, rows, wide), BF)
    outs = pl.pallas_call(
        functools.partial(forward_kernel, loop, stage, len(aliased)),
        out_shape=[jax.ShapeDtypeStruct((rows, width), BF), jax.ShapeDtypeStruct((GROUP, rows, width), BF)]
        + [block] * GROUP,
        in_specs=[ANY] * 3 + [VMEM] * 2 + [ANY] * len(aliased),
        out_specs=[VMEM] + [ANY] * (1 + GROUP),
        scratch_shapes=[
            pltpu.VMEM((GROUP, rows, width), BF),
            pltpu.VMEM((GROUP, rows, wide), BF),
            pltpu.VMEM((rows, width), BF),
            pltpu.VMEM((rows, width), BF),
            pltpu.VMEM((GROUP, width), F32),
        ]
        + [pltpu.SemaphoreType.DMA((GROUP,))] * 3,
        input_output_aliases={5 + j: 2 + j for j in range(len(aliased))},
        compiler_params=pltpu.CompilerParams(vmem_limit_bytes=FWD_MIB << 20),
        cost_estimate=pl.CostEstimate(flops=GROUP * 4 * rows * width * rank, bytes_accessed=GROUP * 4 * width * rank, transcendentals=0),
        name="forward",
    )(x, x0, bias, *pieces, *aliased)
    return outs[0], outs[1], outs[2:]


def run_backward(loop, stage, g, x0, xs, pieces, earlier, total, head=None, extra=None):
    rows, width = g.shape
    rank = pieces[1].shape[1]
    wide = width + rank
    head_too = head is not None
    aliased = () if earlier is None else tuple(earlier)
    block = jax.ShapeDtypeStruct((rows, wide), BF)
    more_in = (head, extra) if head_too else ()
    more_out = [jax.ShapeDtypeStruct((rows, 128), F32)] if head_too else []
    n_out = 1 + len(more_out)
    outs = pl.pallas_call(
        functools.partial(backward_kernel, loop, stage, head_too, total, len(aliased)),
        out_shape=[jax.ShapeDtypeStruct((rows, width), BF)] + more_out + [block] * GROUP,
        in_specs=[ANY] * 3 + [VMEM] * (2 + len(more_in)) + [ANY] * len(aliased),
        out_specs=[VMEM] * n_out + [ANY] * GROUP,
        scratch_shapes=[
            pltpu.VMEM((GROUP, rows, width), BF),
            pltpu.VMEM((GROUP, rows, wide), BF),
            pltpu.VMEM((rows, width), BF),
            pltpu.VMEM((rows, width), BF),
        ]
        + [pltpu.SemaphoreType.DMA((GROUP,))] * 3,
        input_output_aliases={5 + len(more_in) + j: n_out + j for j in range(len(aliased))},
        compiler_params=pltpu.CompilerParams(vmem_limit_bytes=FWD_MIB << 20),
        cost_estimate=pl.CostEstimate(flops=GROUP * 4 * rows * width * rank, bytes_accessed=GROUP * 4 * width * rank, transcendentals=0),
        name="backward",
    )(g, x0, xs, *pieces, *more_in, *aliased)
    return outs[0], (outs[1] if head_too else None), outs[n_out:]


def to_owners(blocks):
    cross = lax.ppermute(blocks[3], ("yl", "core"), [(i, 3 - i) for i in range(4)])
    return [blocks[0], swap(blocks[1], "core"), swap(blocks[2], "yl"), cross]


def to_reps(pieces):
    got = []
    for k in range(1, 8):
        dx, dz = k // 2, k % 2
        pairs = [(x * 2 + z, ((x + dx) % 4) * 2 + (z ^ dz)) for x in range(4) for z in range(2)]
        got.append(lax.ppermute(pieces[k - 1], REP, pairs))
    return got


def rep_at(k, sign):
    x = lax.axis_index("x")
    zl = lax.axis_index("zl")
    return lax.rem(x + sign * (k // 2) + 4, 4) * 2 + lax.rem(zl + k % 2, 2)


def aligned(at, size):
    return pl.ds(at if isinstance(at, int) else pl.multiple_of(at, size), size)


def weight_kernel(loop, direct, *refs):
    ablocks, bblocks = [ref.at[loop] for ref in refs[:GROUP]], refs[GROUP : 2 * GROUP]
    an, ai, bc, bg, gu, gv, gb, sem = refs[-8:]
    outs = refs[2 * GROUP : -8]
    rows, width = ablocks[0].shape[0], an.shape[1]
    rank = ai.shape[1]
    copies = []
    for k in range(GROUP):
        at = pl.ds(k * rows, rows)
        for j, (src, cols, dst) in enumerate(
            (
                (ablocks[k], pl.ds(0, width), an),
                (ablocks[k], pl.ds(width, rank), ai),
                (bblocks[k], pl.ds(0, width), bc),
                (bblocks[k], pl.ds(width, rank), bg),
            )
        ):
            copies.append(pltpu.make_async_copy(src.at[:, cols], dst.at[at, :], sem.at[4 * k + j]))
    for copy in copies:
        copy.start()
    for copy in copies:
        copy.wait()
    step = 256

    @pl.loop(0, width // step)
    def up(j):
        cols = pl.ds(pl.multiple_of(j * step, step), step)
        gu[cols, :] = lax.dot_general(an[:, cols], bg[...], TN, preferred_element_type=F32)
        gv[:, cols] = lax.dot_general(ai[...], bc[:, cols], TN, preferred_element_type=F32)

    bias = jnp.sum(bc[...].astype(F32), axis=0, keepdims=True)
    for i in range(width // 128):
        gb[pl.ds(i, 1), :] = bias[:, i * 128 : (i + 1) * 128]
    per_v, per_u = rank // 8, width // 8
    for k in range(8):
        r, out = (rep_at(k, 1), outs[k]) if direct else (k, outs[0].at[k])
        kind = out.dtype
        out[0:per_v, 0:width] = gv[aligned(r * per_v, per_v), :].astype(kind)
        for j in range(per_u // per_v):
            at = aligned(r * per_u + j * per_v, per_v)
            out[per_v : 2 * per_v, j * rank : (j + 1) * rank] = gu[at, :].astype(kind)
        slim = gb[pl.ds(r * 2, 2), :]
        high = slim.astype(kind).astype(F32)
        packed = jnp.concatenate([high, slim - high, jnp.zeros((2 * per_v - 4, PAD), F32)], axis=0)
        out[:, width:] = packed.astype(kind)


def sum_kernel(width, mine, *refs):
    others, out = refs[:7], refs[7]
    total = mine[...]
    for other in others:
        total = total + other[...].astype(F32)
    out[...] = total.astype(BF)
    slim = total[0:2, width:] + total[2:4, width:]
    high = slim.astype(BF).astype(F32)
    packed = jnp.concatenate([high, slim - high, jnp.zeros((total.shape[0] - 4, PAD), F32)], axis=0)
    out[:, width:] = packed.astype(BF)


def spread_kernel(n_alias, *refs):
    gu, gv, gb = refs[-3:]
    pieces = refs[: len(refs) - 3 - n_alias]
    direct = len(pieces) == 8
    rank, width = gv.shape[1:]
    per_v, per_u = rank // 8, width // 8
    for k in range(8):
        r, piece = (rep_at(k, -1), pieces[k]) if direct else (k, pieces[0].at[k])
        gv[0, aligned(r * per_v, per_v), :] = piece[0:per_v, 0:width].astype(F32)
        for j in range(per_u // per_v):
            at = aligned(r * per_u + j * per_v, per_v)
            gu[0, at, :] = piece[per_v : 2 * per_v, j * rank : (j + 1) * rank].astype(F32)
        slim = piece[:, width:].astype(F32)
        gb[0, pl.ds(r * 2, 2), :] = slim[0:2] + slim[2:4]


def weight_gradients(loop, ablocks, bblocks, loss):
    rows, wide = bblocks[0].shape
    rank = 256
    width = wide - rank
    shape = (2 * rank // 8, width + PAD)
    direct = loop == 0
    if direct:
        out_shape = [jax.ShapeDtypeStruct(shape, F32)] + [jax.ShapeDtypeStruct(shape, BF)] * 7
    else:
        out_shape = [jax.ShapeDtypeStruct((8,) + shape, BF)]
    outs = pl.pallas_call(
        functools.partial(weight_kernel, loop, direct),
        out_shape=out_shape,
        in_specs=[ANY] * (2 * GROUP),
        out_specs=[VMEM] * len(out_shape),
        scratch_shapes=[
            pltpu.VMEM((GROUP * rows, width), BF),
            pltpu.VMEM((GROUP * rows, rank), BF),
            pltpu.VMEM((GROUP * rows, width), BF),
            pltpu.VMEM((GROUP * rows, rank), BF),
            pltpu.VMEM((width, rank), F32),
            pltpu.VMEM((rank, width), F32),
            pltpu.VMEM((width // 128, 128), F32),
            pltpu.SemaphoreType.DMA((4 * GROUP,)),
        ],
        compiler_params=pltpu.CompilerParams(vmem_limit_bytes=14 << 20),
        cost_estimate=pl.CostEstimate(flops=4 * GROUP * rows * width * rank, bytes_accessed=4 * GROUP * rows * wide, transcendentals=0),
        name="weights",
    )(*ablocks, *bblocks)
    if not direct:
        return [lax.psum(outs[0], REP)], None
    outs, loss = lax.optimization_barrier((list(outs), loss))
    for axes in (("yp", "yl"), "core", "x"):
        loss = lax.psum(loss, axes)
    got = to_reps(outs[1:])
    mine = pl.pallas_call(
        functools.partial(sum_kernel, width),
        out_shape=jax.ShapeDtypeStruct(shape, BF),
        in_specs=[VMEM] * 8,
        out_specs=VMEM,
        compiler_params=pltpu.CompilerParams(vmem_limit_bytes=16 << 20),
        name="total",
    )(outs[0], *got)
    return [mine] + to_reps([mine] * 7), loss


def spread(loop, pieces, earlier, loops, width, rank):
    aliased = () if earlier is None else tuple(earlier)
    shapes = [(loops, width, rank), (loops, rank, width), (loops, width // 128, 128)]
    return pl.pallas_call(
        functools.partial(spread_kernel, len(aliased)),
        grid=(1,),
        out_shape=[jax.ShapeDtypeStruct(s, F32) for s in shapes],
        in_specs=[VMEM] * len(pieces) + [ANY] * len(aliased),
        out_specs=[pl.BlockSpec((1,) + s[1:], lambda i: (loop, 0, 0)) for s in shapes],
        input_output_aliases={len(pieces) + j: j for j in range(len(aliased))},
        compiler_params=pltpu.CompilerParams(vmem_limit_bytes=16 << 20),
        name="spread",
    )(*pieces, *aliased)


def local(features, positions, labels, cross_u, cross_v, cross_bias, head, pos_table, hidden_weight, tower_bias, output_weight):
    w_up, w_down, shifts = cross_u[:, 0], cross_v[:, 0], cross_bias[:, 0]
    loops, width, rank = w_up.shape
    micro, rows = features.shape[:2]
    total = float(micro * rows * 8)
    last = (loops - 1, STAGES - 1)
    yl_rows = lax.rem(lax.axis_index("yl") + lax.axis_index("yp"), 2)
    member = yl_rows * 2 + lax.axis_index("core")
    exact = lax.Precision.HIGHEST
    part = micro // GROUP

    u0, v0 = swap(w_up[0], "yl"), swap(w_down[0], "yl")
    uc, vc = swap(w_up, "core"), swap(w_down, "core")
    bias = offset_rows(shifts)
    def mine(value):
        return lax.dynamic_slice_in_dim(value, member * part, part, 0).reshape((part * rows,) + value.shape[2:])

    x0 = z_align(mine(features))
    onehot = (mine(positions)[:, None] == jnp.arange(pos_table.shape[0], dtype=jnp.int32)).astype(F32)
    embedded = jnp.dot(onehot, pos_table, precision=exact)
    hidden = jax.nn.relu(jnp.dot(embedded, hidden_weight, precision=exact) + tower_bias)
    debias = jnp.dot(hidden, output_weight, precision=exact)
    extra = z_align(jnp.stack([debias, mine(labels).astype(F32)], axis=1))
    biases = [bias[:, :, j].reshape(GROUP, width) for j in range(loops)]
    head = head[None]
    up1, down1, u0, v0, biases, x0, extra, head = lax.optimization_barrier((w_up, w_down, u0, v0, biases, x0, extra, head))
    u1, v1 = swap(up1[1], "yl"), swap(down1[1], "yl")

    def pieces_of(loop, u, v):
        return assemble(loop, (w_up, uc, u, swap(u, "core"), w_down, vc, v, swap(v, "core")))

    pieces = [pieces_of(0, u0, v0)]
    x, sent, stash = x0, None, {}
    for loop in range(loops):
        for stage in range(STAGES):
            x, stash[loop, stage], sent = run_forward(loop, stage, x, x0, biases[loop], pieces[loop], sent)
            if (loop, stage) == (0, 3):
                u1, v1, x = lax.optimization_barrier((u1, v1, x))
                pieces.append(pieces_of(1, u1, v1))
            if (loop, stage) != last:
                x = y_hop(x) if stage % 2 == 0 else zy_hop(x)
    ablocks = to_owners(sent)

    g = x
    for loop in reversed(range(loops)):
        sent = None
        for stage in reversed(range(STAGES)):
            more = dict(head=head, extra=extra) if (loop, stage) == last else {}
            g, logit, sent = run_backward(loop, stage, g, x0, stash[loop, stage], pieces[loop], sent, total, **more)
            if more:
                logits = logit[:, 0]
            if (loop, stage) == (1, 0):
                ablocks, g = lax.optimization_barrier((ablocks, g))
            if (loop, stage) == (0, STAGES - 1):
                bblocks, _ = lax.optimization_barrier((bblocks, g))
                upper, _ = weight_gradients(1, ablocks, bblocks, None)
            if (loop, stage) != (0, 0):
                g = y_hop(g) if stage % 2 == 1 else zy_hop(g)
        if loop == 0:
            sent, logits = lax.optimization_barrier((sent, logits))
            loss = jnp.sum(jax.nn.softplus(logits) - extra[:, 1] * logits)
            loss = jnp.where(stage_index() == STAGES - 1, loss, 0.0)
        bblocks = to_owners(sent)
    loss = lax.psum(loss, ("zh", "zl"))
    lower, loss = weight_gradients(0, ablocks, bblocks, loss)
    grads = spread(0, lower, spread(1, upper, None, loops, width, rank), loops, width, rank)
    loss = loss / total
    gu, gv, gb = grads
    return loss, gu[:, None], gv[:, None], gb.reshape(loops, 1, width)


def solution(mesh):
    finer = Mesh(mesh.devices.reshape(2, 2, 2, 2, 4, 2), AXES)
    placed = (
        P(None, REP, None),
        P(None, REP),
        P(None, REP),
        P(None, SECTION, None, None),
        P(None, SECTION, None, None),
        P(None, SECTION, None),
        P(),
        P(),
        P(),
        P(),
        P(),
    )
    return jax.shard_map(
        local,
        mesh=finer,
        in_specs=placed,
        out_specs=(P(), P(None, SECTION, None, None), P(None, SECTION, None, None), P(None, SECTION, None)),
        check_vma=False,
    )
```

```python
import functools

import jax
import jax.numpy as jnp
from jax import lax
from jax.experimental import pallas as pl
from jax.experimental.pallas import tpu as pltpu
from jax.sharding import Mesh
from jax.sharding import PartitionSpec as P

AXES = ("zh", "yp", "yl", "core", "x", "zl")
SECTION = ("zh", "yp", "yl", "core")
REP = ("x", "zl")
EPS = 1e-05
BF = jnp.bfloat16
F32 = jnp.float32
NT = (((1,), (1,)), ((), ()))
TN = (((0,), (0,)), ((), ()))
GROUP = 4
STAGES = 4
PAD = 128
FWD_MIB = 8


ANY = pl.BlockSpec(memory_space=pltpu.HBM)
VMEM = pl.BlockSpec(memory_space=pltpu.VMEM)


def swap(value, axis):
    return lax.ppermute(value, axis, [(0, 1), (1, 0)])


def y_hop(value):
    return lax.ppermute(value, ("yp", "yl"), [(i, 3 - i) for i in range(4)])


def zy_hop(value):
    return lax.ppermute(value, ("zh", "yp", "yl", "zl"), [(i, 15 - i) for i in range(16)])


def z_align(value):
    return lax.ppermute(value, ("zh", "zl"), [(0, 0), (1, 1), (2, 3), (3, 2)])


def offset_rows(own):
    both = jnp.stack([own, swap(own, "yl")])
    return jnp.stack([both, swap(both, "core")], axis=1)


def flip(layer):
    yl = lax.axis_index("yl")
    core = lax.axis_index("core")
    return lax.rem(layer // 2 + yl, 2) * 2 + lax.rem(layer + core, 2)


def assemble_kernel(loop, *refs):
    pieces = refs[: 2 * GROUP]
    u_ref, v_ref, usem, vsem = refs[2 * GROUP :]
    for layer in range(GROUP):
        k = flip(layer)
        for j in range(GROUP):
            u, v = pieces[j], pieces[GROUP + j]
            if j < 2:
                u, v = u.at[loop], v.at[loop]

            @pl.when(k == j)
            def start(u=u, v=v):
                pltpu.make_async_copy(u, u_ref.at[layer], usem.at[layer]).start()
                pltpu.make_async_copy(v, v_ref.at[layer], vsem.at[layer]).start()

    for layer in range(GROUP):
        pltpu.make_async_copy(pieces[2], u_ref.at[layer], usem.at[layer]).wait()
        pltpu.make_async_copy(pieces[GROUP + 2], v_ref.at[layer], vsem.at[layer]).wait()


def assemble(loop, pieces):
    width, rank = pieces[2].shape
    return pl.pallas_call(
        functools.partial(assemble_kernel, loop),
        out_shape=[jax.ShapeDtypeStruct((GROUP, width, rank), BF), jax.ShapeDtypeStruct((GROUP, rank, width), BF)],
        in_specs=[ANY] * (2 * GROUP),
        out_specs=[VMEM] * 2,
        scratch_shapes=[pltpu.SemaphoreType.DMA((GROUP,))] * 2,
        compiler_params=pltpu.CompilerParams(vmem_limit_bytes=12 << 20),
        cost_estimate=pl.CostEstimate(flops=0, bytes_accessed=GROUP * 4 * width * rank, transcendentals=0),
        name="assemble",
    )(*pieces)


def send_block(buf, outs, sems, layer):
    k = flip(layer)
    for j, out in enumerate(outs):

        @pl.when(k == j)
        def start(out=out):
            pltpu.make_async_copy(buf.at[layer], out, sems.at[layer]).start()


def stage_index():
    return lax.axis_index("zh") * 2 + lax.axis_index("yp")


def forward_kernel(loop, stage, n_alias, x_ref, x0_ref, b_ref, *refs):
    u_ref, v_ref = refs[:2]
    refs = refs[2 + n_alias :]
    out_ref, xs_ref = refs[:2]
    blocks = [ref.at[loop] for ref in refs[2 : 2 + GROUP]]
    xsbuf, abuf, xbuf, x0buf, bbuf, xsem, asem, sem = refs[2 + GROUP :]
    width = x_ref.shape[1]

    @pl.when(stage_index() == stage)
    def run():
        copies = [pltpu.make_async_copy(src, dst, sem.at[i]) for i, (src, dst) in enumerate(((x_ref, xbuf), (x0_ref, x0buf), (b_ref, bbuf)))]
        for copy in copies:
            copy.start()
        for copy in copies:
            copy.wait()

        @pl.loop(0, GROUP)
        def step(layer):
            x = xbuf[...]
            xsbuf[layer] = x
            pltpu.make_async_copy(xsbuf.at[layer], xs_ref.at[layer], xsem.at[layer]).start()
            xf = x.astype(F32)
            scale = lax.rsqrt(jnp.mean(xf * xf, axis=-1, keepdims=True) + EPS)
            normed = (xf * scale).astype(BF)
            abuf[layer, :, 0:width] = normed
            inner = jnp.dot(normed, u_ref[layer], preferred_element_type=F32).astype(BF)
            abuf[layer, :, width:] = inner
            send_block(abuf, blocks, asem, layer)
            cross = jnp.dot(inner, v_ref[layer], preferred_element_type=F32) + bbuf[pl.ds(flip(layer), 1), :]
            xbuf[...] = (xf + x0buf[...].astype(F32) * cross).astype(BF)

        out_ref[...] = xbuf[...]

        @pl.loop(0, GROUP)
        def drain(layer):
            pltpu.make_async_copy(xsbuf.at[layer], xs_ref.at[layer], xsem.at[layer]).wait()
            pltpu.make_async_copy(abuf.at[layer], blocks[0], asem.at[layer]).wait()


def backward_kernel(loop, stage, head_too, total, n_alias, g_ref, x0_ref, xs_ref, *refs):
    u_ref, v_ref = refs[:2]
    refs = refs[2:]
    if head_too:
        head_ref, extra_ref = refs[:2]
        refs = refs[2:]
    refs = refs[n_alias:]
    out_ref = refs[0]
    refs = refs[1:]
    if head_too:
        logit_ref = refs[0]
        refs = refs[1:]
    blocks = refs[:GROUP]
    xsbuf, bbuf, gbuf, x0buf, xsem, bsem, sem = refs[GROUP:]
    width = g_ref.shape[1]

    @pl.when(stage_index() == stage)
    def run():
        copies = [pltpu.make_async_copy(g_ref, gbuf, sem.at[0]), pltpu.make_async_copy(x0_ref, x0buf, sem.at[1])]
        for copy in copies:
            copy.start()
        for layer in reversed(range(GROUP)):
            pltpu.make_async_copy(xs_ref.at[layer], xsbuf.at[layer], xsem.at[layer]).start()
        for copy in copies:
            copy.wait()
        if head_too:
            head = head_ref[...]
            logit = jnp.sum(gbuf[...].astype(F32) * head, axis=-1, keepdims=True) + extra_ref[:, 0:1]
            logit_ref[...] = jnp.broadcast_to(logit, logit_ref.shape)
            dlogit = (jax.nn.sigmoid(logit) - extra_ref[:, 1:2]) / total
            gbuf[...] = (dlogit * head).astype(BF)

        @pl.loop(0, GROUP)
        def step(i):
            layer = GROUP - 1 - i
            g = gbuf[...].astype(F32)
            gcross = (g * x0buf[...].astype(F32)).astype(BF)
            bbuf[layer, :, 0:width] = gcross
            ginner = lax.dot_general(gcross, v_ref[layer], NT, preferred_element_type=F32).astype(BF)
            bbuf[layer, :, width:] = ginner
            send_block(bbuf, blocks, bsem, layer)
            gnormed = lax.dot_general(ginner, u_ref[layer], NT, preferred_element_type=F32)
            pltpu.make_async_copy(xs_ref.at[layer], xsbuf.at[layer], xsem.at[layer]).wait()
            xf = xsbuf[layer].astype(F32)
            scale = lax.rsqrt(jnp.mean(xf * xf, axis=-1, keepdims=True) + EPS)
            along = jnp.mean(gnormed * xf, axis=-1, keepdims=True)
            gbuf[...] = (g + scale * gnormed - xf * (scale * scale * scale * along)).astype(BF)

        out_ref[...] = gbuf[...]

        @pl.loop(0, GROUP)
        def drain(layer):
            pltpu.make_async_copy(bbuf.at[layer], blocks[0], bsem.at[layer]).wait()


def run_forward(loop, stage, x, x0, bias, pieces, earlier):
    rows, width = x.shape
    rank = pieces[1].shape[1]
    wide = width + rank
    aliased = () if earlier is None else tuple(earlier)
    block = jax.ShapeDtypeStruct((2, rows, wide), BF)
    outs = pl.pallas_call(
        functools.partial(forward_kernel, loop, stage, len(aliased)),
        out_shape=[jax.ShapeDtypeStruct((rows, width), BF), jax.ShapeDtypeStruct((GROUP, rows, width), BF)]
        + [block] * GROUP,
        in_specs=[ANY] * 3 + [VMEM] * 2 + [ANY] * len(aliased),
        out_specs=[VMEM] + [ANY] * (1 + GROUP),
        scratch_shapes=[
            pltpu.VMEM((GROUP, rows, width), BF),
            pltpu.VMEM((GROUP, rows, wide), BF),
            pltpu.VMEM((rows, width), BF),
            pltpu.VMEM((rows, width), BF),
            pltpu.VMEM((GROUP, width), F32),
        ]
        + [pltpu.SemaphoreType.DMA((GROUP,))] * 3,
        input_output_aliases={5 + j: 2 + j for j in range(len(aliased))},
        compiler_params=pltpu.CompilerParams(vmem_limit_bytes=FWD_MIB << 20),
        cost_estimate=pl.CostEstimate(flops=GROUP * 4 * rows * width * rank, bytes_accessed=GROUP * 4 * width * rank, transcendentals=0),
        name="forward",
    )(x, x0, bias, *pieces, *aliased)
    return outs[0], outs[1], outs[2:]


def run_backward(loop, stage, g, x0, xs, pieces, earlier, total, head=None, extra=None):
    rows, width = g.shape
    rank = pieces[1].shape[1]
    wide = width + rank
    head_too = head is not None
    aliased = () if earlier is None else tuple(earlier)
    block = jax.ShapeDtypeStruct((rows, wide), BF)
    more_in = (head, extra) if head_too else ()
    more_out = [jax.ShapeDtypeStruct((rows, 128), F32)] if head_too else []
    n_out = 1 + len(more_out)
    outs = pl.pallas_call(
        functools.partial(backward_kernel, loop, stage, head_too, total, len(aliased)),
        out_shape=[jax.ShapeDtypeStruct((rows, width), BF)] + more_out + [block] * GROUP,
        in_specs=[ANY] * 3 + [VMEM] * (2 + len(more_in)) + [ANY] * len(aliased),
        out_specs=[VMEM] * n_out + [ANY] * GROUP,
        scratch_shapes=[
            pltpu.VMEM((GROUP, rows, width), BF),
            pltpu.VMEM((GROUP, rows, wide), BF),
            pltpu.VMEM((rows, width), BF),
            pltpu.VMEM((rows, width), BF),
        ]
        + [pltpu.SemaphoreType.DMA((GROUP,))] * 3,
        input_output_aliases={5 + len(more_in) + j: n_out + j for j in range(len(aliased))},
        compiler_params=pltpu.CompilerParams(vmem_limit_bytes=FWD_MIB << 20),
        cost_estimate=pl.CostEstimate(flops=GROUP * 4 * rows * width * rank, bytes_accessed=GROUP * 4 * width * rank, transcendentals=0),
        name="backward",
    )(g, x0, xs, *pieces, *more_in, *aliased)
    return outs[0], (outs[1] if head_too else None), outs[n_out:]


def to_owners(blocks):
    cross = lax.ppermute(blocks[3], ("yl", "core"), [(i, 3 - i) for i in range(4)])
    return [blocks[0], swap(blocks[1], "core"), swap(blocks[2], "yl"), cross]


def to_reps(pieces):
    got = []
    for k in range(1, 8):
        dx, dz = k // 2, k % 2
        pairs = [(x * 2 + z, ((x + dx) % 4) * 2 + (z ^ dz)) for x in range(4) for z in range(2)]
        got.append(lax.ppermute(pieces[k - 1], REP, pairs))
    return got


def rep_at(k, sign):
    x = lax.axis_index("x")
    zl = lax.axis_index("zl")
    return lax.rem(x + sign * (k // 2) + 4, 4) * 2 + lax.rem(zl + k % 2, 2)


def aligned(at, size):
    return pl.ds(at if isinstance(at, int) else pl.multiple_of(at, size), size)


def weight_kernel(loop, direct, *refs):
    ablocks, bblocks = [ref.at[loop] for ref in refs[:GROUP]], refs[GROUP : 2 * GROUP]
    an, ai, bc, bg, gu, gv, gb, sem = refs[-8:]
    outs = refs[2 * GROUP : -8]
    rows, width = ablocks[0].shape[0], an.shape[1]
    rank = ai.shape[1]
    copies = []
    for k in range(GROUP):
        at = pl.ds(k * rows, rows)
        for j, (src, cols, dst) in enumerate(
            (
                (ablocks[k], pl.ds(0, width), an),
                (ablocks[k], pl.ds(width, rank), ai),
                (bblocks[k], pl.ds(0, width), bc),
                (bblocks[k], pl.ds(width, rank), bg),
            )
        ):
            copies.append(pltpu.make_async_copy(src.at[:, cols], dst.at[at, :], sem.at[4 * k + j]))
    for copy in copies:
        copy.start()
    for copy in copies:
        copy.wait()
    step = 256

    @pl.loop(0, width // step)
    def up(j):
        cols = pl.ds(pl.multiple_of(j * step, step), step)
        gu[cols, :] = lax.dot_general(an[:, cols], bg[...], TN, preferred_element_type=F32)
        gv[:, cols] = lax.dot_general(ai[...], bc[:, cols], TN, preferred_element_type=F32)

    bias = jnp.sum(bc[...].astype(F32), axis=0, keepdims=True)
    for i in range(width // 128):
        gb[pl.ds(i, 1), :] = bias[:, i * 128 : (i + 1) * 128]
    per_v, per_u = rank // 8, width // 8
    for k in range(8):
        r, out = (rep_at(k, 1), outs[k]) if direct else (k, outs[0].at[k])
        kind = out.dtype
        out[0:per_v, 0:width] = gv[aligned(r * per_v, per_v), :].astype(kind)
        for j in range(per_u // per_v):
            at = aligned(r * per_u + j * per_v, per_v)
            out[per_v : 2 * per_v, j * rank : (j + 1) * rank] = gu[at, :].astype(kind)
        slim = gb[pl.ds(r * 2, 2), :]
        high = slim.astype(kind).astype(F32)
        packed = jnp.concatenate([high, slim - high, jnp.zeros((2 * per_v - 4, PAD), F32)], axis=0)
        out[:, width:] = packed.astype(kind)


def sum_kernel(width, mine, *refs):
    others, out = refs[:7], refs[7]
    total = mine[...]
    for other in others:
        total = total + other[...].astype(F32)
    out[...] = total.astype(BF)
    slim = total[0:2, width:] + total[2:4, width:]
    high = slim.astype(BF).astype(F32)
    packed = jnp.concatenate([high, slim - high, jnp.zeros((total.shape[0] - 4, PAD), F32)], axis=0)
    out[:, width:] = packed.astype(BF)


def spread_kernel(n_alias, *refs):
    gu, gv, gb = refs[-3:]
    pieces = refs[: len(refs) - 3 - n_alias]
    direct = len(pieces) == 8
    rank, width = gv.shape[1:]
    per_v, per_u = rank // 8, width // 8
    for k in range(8):
        r, piece = (rep_at(k, -1), pieces[k]) if direct else (k, pieces[0].at[k])
        gv[0, aligned(r * per_v, per_v), :] = piece[0:per_v, 0:width].astype(F32)
        for j in range(per_u // per_v):
            at = aligned(r * per_u + j * per_v, per_v)
            gu[0, at, :] = piece[per_v : 2 * per_v, j * rank : (j + 1) * rank].astype(F32)
        slim = piece[:, width:].astype(F32)
        gb[0, pl.ds(r * 2, 2), :] = slim[0:2] + slim[2:4]


def weight_gradients(loop, ablocks, bblocks, loss):
    rows, wide = bblocks[0].shape
    rank = 256
    width = wide - rank
    shape = (2 * rank // 8, width + PAD)
    direct = loop == 0
    if direct:
        out_shape = [jax.ShapeDtypeStruct(shape, F32)] + [jax.ShapeDtypeStruct(shape, BF)] * 7
    else:
        out_shape = [jax.ShapeDtypeStruct((8,) + shape, BF)]
    outs = pl.pallas_call(
        functools.partial(weight_kernel, loop, direct),
        out_shape=out_shape,
        in_specs=[ANY] * (2 * GROUP),
        out_specs=[VMEM] * len(out_shape),
        scratch_shapes=[
            pltpu.VMEM((GROUP * rows, width), BF),
            pltpu.VMEM((GROUP * rows, rank), BF),
            pltpu.VMEM((GROUP * rows, width), BF),
            pltpu.VMEM((GROUP * rows, rank), BF),
            pltpu.VMEM((width, rank), F32),
            pltpu.VMEM((rank, width), F32),
            pltpu.VMEM((width // 128, 128), F32),
            pltpu.SemaphoreType.DMA((4 * GROUP,)),
        ],
        compiler_params=pltpu.CompilerParams(vmem_limit_bytes=14 << 20),
        cost_estimate=pl.CostEstimate(flops=4 * GROUP * rows * width * rank, bytes_accessed=4 * GROUP * rows * wide, transcendentals=0),
        name="weights",
    )(*ablocks, *bblocks)
    if not direct:
        return [lax.psum(outs[0], REP)], None
    outs, loss = lax.optimization_barrier((list(outs), loss))
    got, loss = lax.optimization_barrier((to_reps(outs[1:]), lax.psum(loss, "x")))
    mine = pl.pallas_call(
        functools.partial(sum_kernel, width),
        out_shape=jax.ShapeDtypeStruct(shape, BF),
        in_specs=[VMEM] * 8,
        out_specs=VMEM,
        compiler_params=pltpu.CompilerParams(vmem_limit_bytes=16 << 20),
        name="total",
    )(outs[0], *got)
    mine, loss = lax.optimization_barrier((mine, loss))
    return [mine] + to_reps([mine] * 7), lax.psum(lax.psum(loss, ("yp", "yl")), "core")


def spread(loop, pieces, earlier, loops, width, rank):
    aliased = () if earlier is None else tuple(earlier)
    shapes = [(loops, width, rank), (loops, rank, width), (loops, width // 128, 128)]
    return pl.pallas_call(
        functools.partial(spread_kernel, len(aliased)),
        grid=(1,),
        out_shape=[jax.ShapeDtypeStruct(s, F32) for s in shapes],
        in_specs=[VMEM] * len(pieces) + [ANY] * len(aliased),
        out_specs=[pl.BlockSpec((1,) + s[1:], lambda i: (loop, 0, 0)) for s in shapes],
        input_output_aliases={len(pieces) + j: j for j in range(len(aliased))},
        compiler_params=pltpu.CompilerParams(vmem_limit_bytes=16 << 20),
        name="spread",
    )(*pieces, *aliased)


def local(features, positions, labels, cross_u, cross_v, cross_bias, head, pos_table, hidden_weight, tower_bias, output_weight):
    w_up, w_down, shifts = cross_u[:, 0], cross_v[:, 0], cross_bias[:, 0]
    loops, width, rank = w_up.shape
    micro, rows = features.shape[:2]
    total = float(micro * rows * 8)
    last = (loops - 1, STAGES - 1)
    yl_rows = lax.rem(lax.axis_index("yl") + lax.axis_index("yp"), 2)
    member = yl_rows * 2 + lax.axis_index("core")
    exact = lax.Precision.HIGHEST
    part = micro // GROUP

    u0, v0 = swap(w_up[0], "yl"), swap(w_down[0], "yl")
    uc, vc = swap(w_up, "core"), swap(w_down, "core")
    bias = offset_rows(shifts)
    def mine(value):
        return lax.dynamic_slice_in_dim(value, member * part, part, 0).reshape((part * rows,) + value.shape[2:])

    x0 = z_align(mine(features))
    onehot = (mine(positions)[:, None] == jnp.arange(pos_table.shape[0], dtype=jnp.int32)).astype(F32)
    embedded = jnp.dot(onehot, pos_table, precision=exact)
    hidden = jax.nn.relu(jnp.dot(embedded, hidden_weight, precision=exact) + tower_bias)
    debias = jnp.dot(hidden, output_weight, precision=exact)
    extra = z_align(jnp.stack([debias, mine(labels).astype(F32)], axis=1))
    biases = [bias[:, :, j].reshape(GROUP, width) for j in range(loops)]
    head = head[None]
    up1, down1, u0, v0, biases, x0, extra, head = lax.optimization_barrier((w_up, w_down, u0, v0, biases, x0, extra, head))
    u1, v1 = swap(up1[1], "yl"), swap(down1[1], "yl")

    def pieces_of(loop, u, v):
        return assemble(loop, (w_up, uc, u, swap(u, "core"), w_down, vc, v, swap(v, "core")))

    pieces = [pieces_of(0, u0, v0)]
    x, sent, stash = x0, None, {}
    for loop in range(loops):
        for stage in range(STAGES):
            x, stash[loop, stage], sent = run_forward(loop, stage, x, x0, biases[loop], pieces[loop], sent)
            if (loop, stage) == (0, 3):
                u1, v1, x = lax.optimization_barrier((u1, v1, x))
                pieces.append(pieces_of(1, u1, v1))
            if (loop, stage) != last:
                x = y_hop(x) if stage % 2 == 0 else zy_hop(x)
    ablocks = to_owners(sent)

    g = x
    for loop in reversed(range(loops)):
        sent = None
        for stage in reversed(range(STAGES)):
            more = dict(head=head, extra=extra) if (loop, stage) == last else {}
            g, logit, sent = run_backward(loop, stage, g, x0, stash[loop, stage], pieces[loop], sent, total, **more)
            if more:
                logits = logit[:, 0]
            if (loop, stage) == (1, 0):
                ablocks, g = lax.optimization_barrier((ablocks, g))
            if (loop, stage) == (0, STAGES - 1):
                bblocks, _ = lax.optimization_barrier((bblocks, g))
                upper, _ = weight_gradients(1, ablocks, bblocks, None)
            if (loop, stage) != (0, 0):
                g = y_hop(g) if stage % 2 == 1 else zy_hop(g)
        if loop == 0:
            sent, logits = lax.optimization_barrier((sent, logits))
            loss = jnp.sum(jax.nn.softplus(logits) - extra[:, 1] * logits)
            loss = jnp.where(stage_index() == STAGES - 1, loss, 0.0)
        bblocks = to_owners(sent)
    loss = lax.psum(loss, ("zh", "zl"))
    lower, loss = weight_gradients(0, ablocks, bblocks, loss)
    grads = spread(0, lower, spread(1, upper, None, loops, width, rank), loops, width, rank)
    loss = loss / total
    gu, gv, gb = grads
    return loss, gu[:, None], gv[:, None], gb.reshape(loops, 1, width)


def solution(mesh):
    finer = Mesh(mesh.devices.reshape(2, 2, 2, 2, 4, 2), AXES)
    placed = (
        P(None, REP, None),
        P(None, REP),
        P(None, REP),
        P(None, SECTION, None, None),
        P(None, SECTION, None, None),
        P(None, SECTION, None),
        P(),
        P(),
        P(),
        P(),
        P(),
    )
    return jax.shard_map(
        local,
        mesh=finer,
        in_specs=placed,
        out_specs=(P(), P(None, SECTION, None, None), P(None, SECTION, None, None), P(None, SECTION, None)),
        check_vma=False,
    )
```
